128 devices in a mesh: grid: 2 (over core), pts: 64 (over z, x, y).
Axes of the slice: x: 4, y: 4, z: 4, core: 2. Of those that a mesh axis runs over, the one named last changes fastest.
Arguments:
- spectrum: float32 [2, 28672, 1152], P('grid', 'pts'), may hold values from 0.1 to 1
- interaction: bfloat16 [1152, 1152], replicated, may hold values from -0.1875 to 0.1875
- comp_speed: float32 [2, 1152], replicated, may hold values from -0.45 to 0.45
- sea_mask: int32 [2, 28672], replicated, may hold values 0 or 1
- stokes_kernel: float32 [1152, 80], replicated, may hold values from -0.1875 to 0.1875
- tile_owner: int32 [2, 28672, 1], P('grid', 'pts'), may hold values from 0 to 63; in each aligned block of 448 rows (0 to 447, 448 to 895, ..., all dimensions but the last counted through in order) at most 14 rows name the same one
- ocean_column: int32 [2, 28672], P('grid', 'pts'), may hold values from 0 to 255
- neighbours: int32 [2, 16384, 4], P('grid', 'pts'), may hold values from 0 to 255
- coriolis: float32 [2, 16384], P('grid', 'pts'), may hold values from -1 to 1
- velocity: float32 [2, 2, 40, 16384], P('grid', None, None, 'pts'), may hold values from -6 to 6
Outputs:
- spectrum_next: float32 [2, 28672, 1152], P('grid', 'pts')
- velocity_next: float32 [2, 2, 40, 16384], P('grid', None, None, 'pts')
The draws below stay inside these ranges and needn't reach their ends.
Inputs may be any that keep to these rules, and one draw needn't show every extreme that they name: `tile_owner`: at most 14 of the rows of one device name the same tile, and some tile takes exactly 14 of them.
All inputs are finite; a program needn't handle non-finite values.
Results may differ from the reference program's by a relative error of at most 0.0003.
Values sent between devices are 32-bit elements; how exact they have to be, the bound alone decides.
A program may use at most 128 MiB of HBM per device.

```python
import math
import jax
import jax.numpy as jnp
import numpy as np
from jax import lax

K = 1152
PTS_DEV = 448
GC = 256
LEVELS = 40
COLS = 256
SUBSTEPS = 4
P_SIZE = 28672
CAP = 14
TILES = 16384
N_PTS = 64


def touch_ends(entries, own_key, least, high):
    index_at = [jax.random.randint(jax.random.fold_in(own_key, axis), (), 0, length) for axis, length in enumerate(entries.shape)]
    longest = entries.shape.index(max(entries.shape))
    next_to = index_at[:longest] + [(index_at[longest] + 1) % entries.shape[longest]] + index_at[longest + 1:]
    return entries.at[tuple(index_at)].set(least).at[tuple(next_to)].set(high)


def level_of(rng, shape, cuts, low, top_value):
    def one(axis_at, shards_of):
        heights = jax.random.uniform(jax.random.fold_in(jax.random.fold_in(rng, 6), axis_at), (shards_of,), jnp.float32, low / len(cuts), top_value / len(cuts))
        return jnp.repeat(jnp.exp(heights), shape[axis_at] // shards_of).reshape((-1,) + (1,) * (len(shape) - axis_at - 1))

    gain = one(*cuts[0])
    for cut in cuts[1:]:
        gain = gain * one(*cut)
    return gain


def deal_out(stream_key, own, number, rows, amount, top, most, lean):
    sequence = jax.random.permutation(stream_key, amount)
    packed, usual = portions_of(amount, rows * top, most, lean, True), portions_of(amount, rows * top, most, lean, False)
    places = jnp.arange(amount)

    def named(lengths, rotation):
        used = int((lengths > 0).sum())
        fixed = max(1, used // 4)
        passed = fixed + (places - fixed + rotation * (used - fixed)) % max(1, amount - fixed)
        return jnp.zeros((amount,), jnp.int32).at[sequence[jnp.where(places < fixed, places, passed)]].set(jnp.asarray(lengths, jnp.int32))

    lengths = jnp.where(number % 4 == 0, named(packed, number // 4), named(usual, number - number // 4 - 1))
    mixed = jax.random.permutation(jax.random.fold_in(own, 3), amount)
    giver, taker = mixed[0:amount // 2 * 2:2], mixed[1:amount // 2 * 2:2]
    slack = jnp.minimum(lengths[giver] - 1, most - lengths[taker]) // 2
    slack = jnp.where((giver == sequence[0]) | (taker == sequence[0]) | (lengths[taker] == 0), 0, jnp.maximum(slack, 0))
    passed = jax.random.randint(jax.random.fold_in(own, 4), (amount // 2,), 0, 1 << 20) % (slack + 1)
    lengths = lengths.at[giver].add(-passed).at[taker].add(passed)
    labels = jnp.searchsorted(jnp.cumsum(lengths), jnp.arange(rows * top), side="right").astype(jnp.int32)
    grid = labels.reshape(top, rows).T
    grid = grid[jax.random.permutation(jax.random.fold_in(own, 1), rows)]
    rotation = jax.random.randint(jax.random.fold_in(own, 2), (rows, 1), 0, top)
    return jnp.take_along_axis(grid, (jnp.arange(top)[None, :] + rotation) % top, axis=1)


def portions_of(number_of, total, reach, skew, full):
    loads = [(1 << 20) // math.isqrt(grade ** skew) + 1 for grade in range(1, number_of + 1)]
    largest = reach if full else min(reach, max(-(-total // number_of), total * loads[0] // sum(loads)))
    least = 1 if total - largest >= number_of - 1 else 0
    holding, rest = [largest] + [least] * (number_of - 1), total - largest - least * (number_of - 1)
    while rest > 0:
        candidates = [i for i in range(1, number_of) if holding[i] < largest] or [i for i in range(1, number_of) if holding[i] < reach]
        whole, left = sum([loads[i] for i in candidates]), rest
        for i in candidates:
            more = min(reach - holding[i], max(1, left * loads[i] // whole), rest)
            holding[i] = holding[i] + more
            rest = rest - more
    return np.array(holding)


def centred(stream_key, dims, scale, bound, shards=(), kind=jnp.bfloat16):
    gain = level_of(stream_key, dims, shards, -0.22, 0.18) if shards else 1.0
    array = jax.random.normal(stream_key, dims, jnp.float32) * scale * gain
    return jnp.minimum(jnp.maximum(array, -bound), bound).astype(kind)


def setup_inputs(seed: int = 0) -> dict:
    arg_keys = jax.random.split(jax.random.key(seed), 11)
    spectrum = jnp.clip(jnp.exp(math.log(1.0) - 2.3025851 * jax.random.uniform(arg_keys[0], (2, P_SIZE, K), jnp.float32) ** level_of(arg_keys[0], (2, P_SIZE, K), ((0, 2), (1, 64)), -0.2, 0.2)), 0.1, 1.0)
    interaction = centred(arg_keys[1], (K, K), K ** -0.5, 0.1875)
    comp_speed = jnp.clip(jax.random.uniform(arg_keys[2], (2, K), jnp.float32, -0.45, 0.45), -0.45, 0.45)
    sea_mask = touch_ends((jax.random.randint(arg_keys[3], (2, P_SIZE), 0, 5) < 4).astype(jnp.int32), jax.random.fold_in(arg_keys[3], 1), 0, 1)
    stokes_kernel = centred(arg_keys[4], (K, 2 * LEVELS), K ** -0.5, 0.1875, (), jnp.float32)
    tile_owner_keys = jax.random.split(jax.random.fold_in(arg_keys[5], 1), 2 * P_SIZE // PTS_DEV)
    tile_owner_turns = jax.random.permutation(jax.random.fold_in(arg_keys[5], 3), 2 * P_SIZE // PTS_DEV)
    tile_owner = jax.vmap(lambda own, number: deal_out(jax.random.fold_in(arg_keys[5], 2), own, number, PTS_DEV, N_PTS, 1, CAP, 2))(tile_owner_keys, tile_owner_turns).reshape((2, P_SIZE, 1))
    ocean_column = touch_ends(jax.random.randint(arg_keys[6], (2, P_SIZE), 0, COLS), jax.random.fold_in(arg_keys[6], 1), 0, COLS - 1).astype(jnp.int32)
    neighbours = touch_ends(jax.random.randint(arg_keys[7], (2, TILES, 4), 0, COLS), jax.random.fold_in(arg_keys[7], 1), 0, COLS - 1).astype(jnp.int32)
    coriolis = jnp.clip(jax.random.uniform(arg_keys[8], (2, TILES), jnp.float32, -1.0, 1.0) * level_of(arg_keys[8], (2, TILES), ((0, 2), (1, 64)), -0.4, 0.0), -1.0, 1.0)
    velocity = centred(arg_keys[9], (2, 2, LEVELS, TILES), 1.0, 6.0, ((0, 2), (3, 64)), jnp.float32)
    return {"spectrum": spectrum, "interaction": interaction, "comp_speed": comp_speed, "sea_mask": sea_mask, "stokes_kernel": stokes_kernel, "tile_owner": tile_owner, "ocean_column": ocean_column, "neighbours": neighbours, "coriolis": coriolis, "velocity": velocity}


def advect(field, speed_x, speed_y, mask, top, bottom):
    upper = jnp.concatenate([top[:, None, :], field[:, :-1]], axis=1)
    lower = jnp.concatenate([field[:, 1:], bottom[:, None, :]], axis=1)
    zeros = jnp.zeros_like(field[:, :, :1])
    left = jnp.concatenate([zeros, field[:, :, :-1]], axis=2)
    right = jnp.concatenate([field[:, :, 1:], zeros], axis=2)
    sx = speed_x[:, None, None]
    sy = speed_y[:, None, None]
    result = field - jnp.maximum(sx, 0.0) * (field - upper) - jnp.minimum(sx, 0.0) * (lower - field)
    result = result - jnp.maximum(sy, 0.0) * (field - left) - jnp.minimum(sy, 0.0) * (right - field)
    return result * mask


def reference(spectrum, interaction, comp_speed, sea_mask, stokes_kernel, tile_owner, ocean_column, neighbours, coriolis, velocity):
    points = spectrum.shape[1]
    comps = spectrum.shape[2]
    rows = points // GC
    held = points // N_PTS
    flat = spectrum.reshape(2 * points, comps)
    mix = jnp.dot(flat.astype(jnp.bfloat16), interaction, preferred_element_type=jnp.float32)
    relaxed = (flat + 0.5 * flat * jnp.tanh(mix)).reshape(2, N_PTS, held, comps)
    placed = jnp.transpose(relaxed, (0, 2, 1, 3)).reshape(2 * points, comps)
    stacked = placed.T.reshape(N_PTS, comps // N_PTS, 2 * rows, GC)
    speeds = comp_speed.reshape(2, N_PTS, comps // N_PTS)
    mask = sea_mask.reshape(2 * rows, GC).astype(jnp.float32)

    def block(item):
        field, speed_x, speed_y = item
        edge = jnp.zeros((field.shape[0], GC), jnp.float32)
        for step in range(SUBSTEPS):
            field = advect(field, speed_x, speed_y, mask, edge, edge)
        return field

    moved = lax.map(block, (stacked, speeds[0], speeds[1]))
    moved = moved.reshape(comps, 2 * points).T.reshape(2, held, N_PTS, comps)
    spectrum_next = jnp.transpose(moved, (0, 2, 1, 3)).reshape(2, points, comps)
    outs = []
    for g in range(2):
        stokes = jnp.dot(spectrum_next[g], stokes_kernel, precision=lax.Precision.HIGHEST, preferred_element_type=jnp.float32)
        ident = tile_owner[g, :, 0] * COLS + ocean_column[g]
        total = N_PTS * COLS
        drift_sum = jax.ops.segment_sum(stokes, ident, total)
        count = jax.ops.segment_sum(jnp.ones((points,), jnp.float32), ident, total)
        drift = (drift_sum / jnp.maximum(count, 1.0)[:, None]).T
        east_drift = drift[:LEVELS]
        north_drift = drift[LEVELS:]
        base = (jnp.arange(total, dtype=jnp.int32) // COLS * COLS)[:, None]
        near = neighbours[g] + base
        east_flow = velocity[g, 0]
        north_flow = velocity[g, 1]
        zeta = (north_flow[:, near[:, 0]] - north_flow[:, near[:, 1]]) - (east_flow[:, near[:, 2]] - east_flow[:, near[:, 3]])
        spin = coriolis[g][None, :]
        new_east = east_flow + 0.25 * (spin * north_flow + (spin + zeta) * north_drift)
        new_north = north_flow - 0.25 * (spin * east_flow + (spin + zeta) * east_drift)
        outs.append(jnp.stack([new_east, new_north]))
    return spectrum_next, jnp.stack(outs)
```

```python
import jax
import jax.numpy as jnp
from jax import lax
from jax.experimental import pallas as pl
from jax.experimental.pallas import tpu as pltpu
from jax.sharding import PartitionSpec as P

MESH = pl.DeviceIdType.MESH
LANES = 128
SUB = 8
SIDE = 4
GC = 256


def wave_kernel(
    spec_hbm,
    inter_hbm,
    speed,
    sea,
    kern,
    out_hbm,
    stokes,
    spec,
    inter,
    half,
    sent,
    own,
    left,
    right,
    wide,
    swept,
    back,
    home,
    final,
    mask_pos,
    mask_neg,
    mask_now,
    load_sem,
    store_sem,
    in_send,
    in_recv,
    halo_send,
    halo_recv,
    edge_send,
    edge_recv,
    out_send,
    out_recv,
):
    chunks = spec.shape[0]
    held = spec.shape[1]
    rows = held // SIDE
    tall = rows + 2 * SIDE
    grid = lax.axis_index("grid")
    place = lax.axis_index("pts")
    y = lax.rem(place, SIDE)
    base = place - y
    block = 16 * y + place // SIDE
    after = lax.rem(block + 1, 64)
    before = lax.rem(block + 63, 64)
    after_dev = SIDE * lax.rem(after, 16) + after // 16
    before_dev = SIDE * lax.rem(before, 16) + before // 16
    peers = [base + lax.rem(y + d, SIDE) for d in (1, 2, 3)]
    lanes = lambda k: pl.ds(pl.multiple_of(k * LANES, LANES), LANES)

    def load(k):
        return (
            pltpu.make_async_copy(spec_hbm.at[:, lanes(k)], spec.at[k], load_sem.at[0, k]),
            pltpu.make_async_copy(inter_hbm.at[:, lanes(k)], inter.at[k], load_sem.at[1, k]),
        )

    @pl.loop(0, chunks)
    def _(k):
        load(k)[0].start()

    @pl.loop(0, chunks)
    def _(k):
        load(k)[1].start()

    barrier = pltpu.get_barrier_semaphore()
    for peer in peers + [after_dev, before_dev]:
        pl.semaphore_signal(barrier, inc=1, device_id={"pts": peer}, device_id_type=MESH)
    pl.semaphore_signal(barrier, inc=1, device_id={"grid": 1 - grid}, device_id_type=MESH)
    pl.semaphore_wait(barrier, 6)

    for k in range(chunks):
        load(k)[0].wait()
        for m in range(SIDE):
            half[m * rows : (m + 1) * rows, k * LANES : (k + 1) * LANES] = spec[
                k, pl.ds(m, rows, stride=SIDE), :
            ].astype(jnp.bfloat16)

    row_at = lax.broadcasted_iota(jnp.int32, (tall, 2 * rows), 0) + (rows * grid - SIDE)
    row_of = lax.broadcasted_iota(jnp.int32, (tall, 2 * rows), 1)
    picked = jnp.dot(
        (row_at == row_of).astype(jnp.bfloat16),
        sea[...].astype(jnp.bfloat16),
        preferred_element_type=jnp.float32,
    ).astype(jnp.bfloat16)
    column = lax.broadcasted_iota(jnp.int32, (GC, LANES), 0)
    for s in range(SUB):
        first = (column == SIDE * block - SIDE + s).astype(jnp.bfloat16)
        second = (column == SIDE * block + 7 - s).astype(jnp.bfloat16)
        mask_pos[pl.ds(s, tall, stride=SUB), :] = jnp.dot(
            picked, first, preferred_element_type=jnp.float32
        )
        mask_neg[pl.ds(s, tall, stride=SUB), :] = jnp.dot(
            picked, second, preferred_element_type=jnp.float32
        )

    def send_in(k, d):
        return pltpu.make_async_remote_copy(
            src_ref=sent.at[k, lax.rem(y + d, SIDE)],
            dst_ref=own.at[k, y],
            send_sem=in_send.at[k, d - 1],
            recv_sem=in_recv.at[k, d - 1],
            device_id={"pts": peers[d - 1]},
            device_id_type=MESH,
        )

    def send_halo(k, side):
        return pltpu.make_async_remote_copy(
            src_ref=own.at[k],
            dst_ref=(left if side == 0 else right).at[k],
            send_sem=halo_send.at[k, side],
            recv_sem=halo_recv.at[k, side],
            device_id={"pts": after_dev if side == 0 else before_dev},
            device_id_type=MESH,
        )

    def send_edge(k):
        at = pl.multiple_of((rows - (rows - SIDE) * grid) * SUB, SUB)
        to = pl.multiple_of((rows + SIDE) * SUB * grid, SUB)
        return pltpu.make_async_remote_copy(
            src_ref=wide.at[k, pl.ds(at, SIDE * SUB)],
            dst_ref=wide.at[k, pl.ds(to, SIDE * SUB)],
            send_sem=edge_send.at[k],
            recv_sem=edge_recv.at[k],
            device_id={"grid": 1 - grid},
            device_id_type=MESH,
        )

    def send_out(k, d):
        return pltpu.make_async_remote_copy(
            src_ref=back.at[k, lax.rem(y + d, SIDE)],
            dst_ref=home.at[k, y],
            send_sem=out_send.at[k, d - 1],
            recv_sem=out_recv.at[k, d - 1],
            device_id={"pts": peers[d - 1]},
            device_id_type=MESH,
        )

    def store(k):
        return pltpu.make_async_copy(final.at[k], out_hbm.at[:, lanes(k)], store_sem.at[k])

    def relax(k):
        load(k)[1].wait()
        mix = jnp.dot(half[...], inter[k], preferred_element_type=jnp.float32)
        grown = jnp.tanh(mix)
        for m in range(SIDE):
            local = spec[k, pl.ds(m, rows, stride=SIDE), :]
            sent[k, m] = local + 0.5 * local * grown[m * rows : (m + 1) * rows]
        own[k, y] = sent[k, y]
        for d in (2, 1, 3):
            send_in(k, d).start()

    def positive(k):
        return speed[1:2, lanes(k)] > 0.0

    def assemble(k):
        pos = jnp.broadcast_to(positive(k), (rows, LANES))
        from_left = block > 0
        from_right = block < 63
        for s in range(SIDE):
            lower = jnp.where(from_left, left[k, s], 0.0)
            upper = jnp.where(from_right, right[k, SIDE - 1 - s], 0.0)
            wide[k, pl.ds(SIDE * SUB + s, rows, stride=SUB), :] = jnp.where(pos, lower, upper)
        for q in range(SIDE):
            wide[k, pl.ds(SIDE * SUB + SIDE + q, rows, stride=SUB), :] = jnp.where(
                pos, own[k, q], own[k, SIDE - 1 - q]
            )
        outside = pl.multiple_of((rows + SIDE) * SUB * grid, SUB)
        wide[k, pl.ds(outside, SIDE * SUB), :] = jnp.zeros((SIDE * SUB, LANES), jnp.float32)

    def sweep(k):
        spread = lambda v: jnp.broadcast_to(v, (SUB, LANES))
        cx = speed[0:1, lanes(k)]
        cy = speed[1:2, lanes(k)]
        down_rate = spread(jnp.maximum(cx, 0.0))
        up_rate = spread(jnp.maximum(-cx, 0.0))
        side_rate = spread(jnp.abs(cy))
        keep = 1.0 - down_rate - up_rate - side_rate
        pos = spread(cy) > 0.0

        @pl.loop(0, tall // SUB)
        def _(part):
            for u in range(SUB):
                at = pl.ds(pl.multiple_of((part * SUB + u) * SUB, SUB), SUB)
                mask_now[at, :] = jnp.where(pos, mask_pos[at, :], mask_neg[at, :])

        zero = jnp.zeros((SUB, LANES), jnp.float32)

        def part(i, carry):
            held_rows = [list(pair) for pair in carry[0]]
            masks = list(carry[1])
            for u in range(SUB):
                at = pl.ds(pl.multiple_of((i * SUB + u) * SUB, SUB), SUB)
                value = wide[k, at, :]
                for stage in range(SIDE):
                    previous, current = held_rows[stage]
                    moved = (
                        keep * current
                        + down_rate * previous
                        + up_rate * value
                        + side_rate * pltpu.roll(current, 1, 0)
                    )
                    held_rows[stage] = [current, value]
                    value = moved * masks[stage]
                swept[at, :] = value
                masks = [mask_now[at, :]] + masks[: SIDE - 1]
            return tuple(tuple(pair) for pair in held_rows), tuple(masks)

        start = (tuple((zero, zero) for _ in range(SIDE)), (zero,) * SIDE)
        lax.fori_loop(0, tall // SUB, part, start)
        wanted = jnp.broadcast_to(cy > 0.0, (rows, LANES))
        columns = [
            swept[pl.ds(2 * SIDE * SUB + SIDE + q, rows, stride=SUB), :] for q in range(SIDE)
        ]
        for c in range(SIDE):
            back[k, c] = jnp.where(wanted, columns[c], columns[SIDE - 1 - c])
        home[k, y] = back[k, y]
        for d in (2, 1, 3):
            send_out(k, d).start()

    def finish(k):
        for m in range(SIDE):
            final[k, pl.ds(m, rows, stride=SIDE), :] = home[k, m]
        store(k).start()
        stokes[...] += jnp.dot(
            final[k],
            kern[k],
            precision=lax.Precision.HIGHEST,
            preferred_element_type=jnp.float32,
        )

    stokes[...] = jnp.zeros_like(stokes)
    ahead = 2
    for k in range(ahead):
        relax(k)

    @pl.loop(0, chunks + 3)
    def _(t):
        @pl.when(t + ahead < chunks)
        def _():
            relax(t + ahead)

        @pl.when(t < chunks)
        def _():
            for d in (1, 2, 3):
                send_in(t, d).wait_recv()
            for side in range(2):
                send_halo(t, side).start()

        @pl.when((t >= 1) & (t < chunks + 1))
        def _():
            k = t - 1
            for side in range(2):
                send_halo(k, side).wait_recv()
            assemble(k)
            send_edge(k).start()

        @pl.when((t >= 2) & (t < chunks + 2))
        def _():
            k = t - 2
            send_edge(k).wait_recv()
            sweep(k)

        @pl.when(t >= 3)
        def _():
            k = t - 3
            for d in (1, 2, 3):
                send_out(k, d).wait_recv()
            finish(k)

    @pl.loop(0, chunks)
    def _(k):
        for d in (1, 2, 3):
            send_in(k, d).wait_send()
            send_out(k, d).wait_send()
        for side in range(2):
            send_halo(k, side).wait_send()
        send_edge(k).wait_send()
        store(k).wait()


def wave_step(spectrum, interaction, comp_speed, sea, stokes_kernel):
    held, comps = spectrum.shape
    chunks = comps // LANES
    rows = held // SIDE
    tall = rows + 2 * SIDE
    f32 = jnp.float32
    piece = pltpu.VMEM((chunks, SIDE, rows, LANES), f32)
    vmem = pl.BlockSpec(memory_space=pltpu.VMEM)
    anywhere = pl.BlockSpec(memory_space=pl.ANY)
    dma = pltpu.SemaphoreType.DMA
    return pl.pallas_call(
        wave_kernel,
        out_shape=(
            jax.ShapeDtypeStruct((held, comps), f32),
            jax.ShapeDtypeStruct((held, LANES), f32),
        ),
        in_specs=[anywhere, anywhere, vmem, vmem, vmem],
        out_specs=(anywhere, vmem),
        scratch_shapes=[
            pltpu.VMEM((chunks, held, LANES), f32),
            pltpu.VMEM((chunks, comps, LANES), jnp.bfloat16),
            pltpu.VMEM((held, comps), jnp.bfloat16),
            piece,
            piece,
            piece,
            piece,
            pltpu.VMEM((chunks, tall * SUB, LANES), f32),
            pltpu.VMEM((tall * SUB, LANES), f32),
            piece,
            piece,
            pltpu.VMEM((chunks, held, LANES), f32),
            pltpu.VMEM((tall * SUB, LANES), f32),
            pltpu.VMEM((tall * SUB, LANES), f32),
            pltpu.VMEM((tall * SUB, LANES), f32),
            dma((2, chunks)),
            dma((chunks,)),
            dma((chunks, 3)),
            dma((chunks, 3)),
            dma((chunks, 2)),
            dma((chunks, 2)),
            dma((chunks,)),
            dma((chunks,)),
            dma((chunks, 3)),
            dma((chunks, 3)),
        ],
        compiler_params=pltpu.CompilerParams(
            collective_id=0, has_side_effects=True, vmem_limit_bytes=56 << 20
        ),
        name="wave_step",
    )(spectrum, interaction, comp_speed, sea, stokes_kernel)


def select_columns(flow, chosen):
    columns = flow.shape[1]
    picker = (jnp.arange(columns, dtype=jnp.int32)[:, None] == chosen[None, :]).astype(jnp.float32)
    return jnp.dot(
        flow, picker, precision=lax.Precision.HIGHEST, preferred_element_type=jnp.float32
    )


def per_device(
    spectrum,
    interaction,
    comp_speed,
    sea_mask,
    stokes_kernel,
    tile_owner,
    ocean_column,
    neighbours,
    coriolis,
    velocity,
):
    local = spectrum[0]
    held, comps = local.shape
    sea = sea_mask.reshape(-1, GC)
    wide_kernel = jnp.pad(stokes_kernel, ((0, 0), (0, LANES - stokes_kernel.shape[1])))
    spectrum_next, stokes = wave_step(
        local, interaction, comp_speed, sea, wide_kernel.reshape(-1, LANES, LANES)
    )
    stokes = stokes[:, : stokes_kernel.shape[1]]
    tiles = lax.axis_size("pts")
    capacity = 2 * held // tiles
    owner = tile_owner[0, :, 0]
    position = jnp.arange(held, dtype=jnp.int32)
    earlier = (owner[:, None] == owner[None, :]) & (position[None, :] < position[:, None])
    rank = jnp.sum(earlier.astype(jnp.int32), axis=1)
    slot = owner * capacity + rank
    placer = (slot[:, None] == jnp.arange(tiles * capacity, dtype=jnp.int32)[None, :]).astype(
        jnp.float32
    )
    payload = jnp.concatenate([stokes, (ocean_column[0] + 1)[:, None].astype(jnp.float32)], axis=1)
    buffer = jnp.dot(
        placer.T, payload, precision=lax.Precision.HIGHEST, preferred_element_type=jnp.float32
    )
    buffer = buffer.reshape(tiles, capacity, payload.shape[1])
    received = lax.all_to_all(buffer, "pts", split_axis=0, concat_axis=0, tiled=True).reshape(
        tiles * capacity, payload.shape[1]
    )
    columns = coriolis.shape[1]
    target = received[:, -1].astype(jnp.int32) - 1
    onehot = (jnp.arange(columns, dtype=jnp.int32)[:, None] == target[None, :]).astype(jnp.float32)
    drift_sum = jnp.dot(
        onehot,
        received[:, :-1],
        precision=lax.Precision.HIGHEST,
        preferred_element_type=jnp.float32,
    )
    count = jnp.sum(onehot, axis=1)
    drift = (drift_sum / jnp.maximum(count, 1.0)[:, None]).T
    levels = drift.shape[0] // 2
    east_drift = drift[:levels]
    north_drift = drift[levels:]
    near = neighbours[0]
    east_flow = velocity[0, 0]
    north_flow = velocity[0, 1]
    zeta = (
        select_columns(north_flow, near[:, 0])
        - select_columns(north_flow, near[:, 1])
        - (select_columns(east_flow, near[:, 2]) - select_columns(east_flow, near[:, 3]))
    )
    spin = coriolis[0][None, :]
    new_east = east_flow + 0.25 * (spin * north_flow + (spin + zeta) * north_drift)
    new_north = north_flow - 0.25 * (spin * east_flow + (spin + zeta) * east_drift)
    return (spectrum_next[None], jnp.stack([new_east, new_north])[None])


def solution(mesh):
    placed = (
        P("grid", "pts", None),
        P(),
        P(),
        P(),
        P(),
        P("grid", "pts", None),
        P("grid", "pts"),
        P("grid", "pts", None),
        P("grid", "pts"),
        P("grid", None, None, "pts"),
    )
    return jax.shard_map(
        per_device,
        mesh=mesh,
        in_specs=placed,
        out_specs=(P("grid", "pts", None), P("grid", None, None, "pts")),
        check_vma=False,
    )
```

```python
import jax
import jax.numpy as jnp
from jax import lax
from jax.experimental import pallas as pl
from jax.experimental.pallas import tpu as pltpu
from jax.sharding import PartitionSpec as P

MESH = pl.DeviceIdType.MESH
LANES = 128
SUB = 8
SIDE = 4
GC = 256


def wave_kernel(
    spec_hbm,
    inter_hbm,
    speed,
    sea,
    kern,
    owner,
    ocean,
    near,
    coriolis,
    velocity,
    out_hbm,
    velocity_out,
    spec,
    inter,
    half,
    sent,
    own,
    left,
    right,
    wide,
    swept,
    back,
    home,
    final,
    mask_pos,
    mask_neg,
    mask_now,
    sea_rows,
    drift_kernel,
    stokes,
    placer,
    zeta,
    posted,
    arrived,
    load_sem,
    store_sem,
    in_send,
    in_recv,
    halo_send,
    halo_recv,
    edge_send,
    edge_recv,
    out_send,
    out_recv,
    post_send,
    post_recv,
):
    f32, bf16, i32 = jnp.float32, jnp.bfloat16, jnp.int32
    chunks, held = spec.shape[:2]
    rows = held // SIDE
    tall = rows + 2 * SIDE
    tiles, slots = arrived.shape[:2]
    drifts = kern.shape[1]
    levels = drifts // 2
    cols = coriolis.shape[1]
    grid = lax.axis_index("grid")
    place = lax.axis_index("pts")
    y = lax.rem(place, SIDE)
    base = place - y
    block = 16 * y + place // SIDE
    after = lax.rem(block + 1, 64)
    before = lax.rem(block + 63, 64)
    after_dev = SIDE * lax.rem(after, 16) + after // 16
    before_dev = SIDE * lax.rem(before, 16) + before // 16
    peers = [base + lax.rem(y + d, SIDE) for d in (1, 2, 3)]
    lanes = lambda k: pl.ds(pl.multiple_of(k * LANES, LANES), LANES)

    def load_spec(k):
        return pltpu.make_async_copy(spec_hbm.at[:, lanes(k)], spec.at[k], load_sem.at[0, k])

    def load_inter(k):
        return pltpu.make_async_copy(inter_hbm.at[:, lanes(k)], inter.at[k], load_sem.at[1, k])

    barrier = pltpu.get_barrier_semaphore()

    @pl.loop(1, tiles)
    def _(d):
        pl.semaphore_signal(
            barrier, inc=1, device_id={"pts": lax.rem(place + d, tiles)}, device_id_type=MESH
        )

    pl.semaphore_signal(barrier, inc=1, device_id={"grid": 1 - grid}, device_id_type=MESH)

    @pl.loop(0, chunks)
    def _(k):
        load_spec(k).start()

    @pl.loop(0, chunks)
    def _(k):
        load_inter(k).start()

    for k in range(chunks):
        load_spec(k).wait()
        for m in range(SIDE):
            half[m * rows : (m + 1) * rows, k * LANES : (k + 1) * LANES] = spec[
                k, pl.ds(m, rows, stride=SIDE), :
            ].astype(bf16)

    def send_in(k, d):
        return pltpu.make_async_remote_copy(
            src_ref=sent.at[k, lax.rem(y + d, SIDE)],
            dst_ref=own.at[k, y],
            send_sem=in_send.at[k, d - 1],
            recv_sem=in_recv.at[k, d - 1],
            device_id={"pts": peers[d - 1]},
            device_id_type=MESH,
        )

    def send_halo(k, side):
        return pltpu.make_async_remote_copy(
            src_ref=own.at[k],
            dst_ref=(left if side == 0 else right).at[k],
            send_sem=halo_send.at[k, side],
            recv_sem=halo_recv.at[k, side],
            device_id={"pts": after_dev if side == 0 else before_dev},
            device_id_type=MESH,
        )

    def send_edge(k):
        at = pl.multiple_of((rows - (rows - SIDE) * grid) * SUB, SUB)
        to = pl.multiple_of((rows + SIDE) * SUB * grid, SUB)
        return pltpu.make_async_remote_copy(
            src_ref=wide.at[k, pl.ds(at, SIDE * SUB)],
            dst_ref=wide.at[k, pl.ds(to, SIDE * SUB)],
            send_sem=edge_send.at[k],
            recv_sem=edge_recv.at[k],
            device_id={"grid": 1 - grid},
            device_id_type=MESH,
        )

    def send_out(k, d):
        return pltpu.make_async_remote_copy(
            src_ref=back.at[k, lax.rem(y + d, SIDE)],
            dst_ref=home.at[k, y],
            send_sem=out_send.at[k, d - 1],
            recv_sem=out_recv.at[k, d - 1],
            device_id={"pts": peers[d - 1]},
            device_id_type=MESH,
        )

    def post(d):
        peer = lax.rem(place + d, tiles)
        return pltpu.make_async_remote_copy(
            src_ref=posted.at[peer],
            dst_ref=arrived.at[place],
            send_sem=post_send,
            recv_sem=post_recv,
            device_id={"pts": peer},
            device_id_type=MESH,
        )

    def store(k):
        return pltpu.make_async_copy(final.at[k], out_hbm.at[:, lanes(k)], store_sem.at[k])

    def relax(k):
        load_inter(k).wait()
        mix = jnp.dot(half[...], inter[k], preferred_element_type=f32)
        grown = jnp.tanh(mix)
        for m in range(SIDE):
            local = spec[k, pl.ds(m, rows, stride=SIDE), :]
            sent[k, m] = local + 0.5 * local * grown[m * rows : (m + 1) * rows]
        own[k, y] = sent[k, y]

    def launch(k):
        for d in (2, 1, 3):
            send_in(k, d).start()

    def forward(k):
        for d in (1, 2, 3):
            send_in(k, d).wait_recv()
        for side in range(2):
            send_halo(k, side).start()

    def prepare_masks():
        @pl.loop(0, rows)
        def _(r):
            pair = sea[:, pl.ds(pl.multiple_of(r * GC, GC), GC)].astype(f32)
            sea_rows[pl.ds(r, 1), :] = pair[0:1]
            sea_rows[pl.ds(r + rows, 1), :] = pair[1:2]

        row_at = lax.broadcasted_iota(i32, (tall, 2 * rows), 0) + (rows * grid - SIDE)
        row_of = lax.broadcasted_iota(i32, (tall, 2 * rows), 1)
        picked = jnp.dot(
            (row_at == row_of).astype(bf16),
            sea_rows[...].astype(bf16),
            preferred_element_type=f32,
        ).astype(bf16)
        column = lax.broadcasted_iota(i32, (GC, LANES), 0)
        for s in range(SUB):
            first = (column == SIDE * block - SIDE + s).astype(bf16)
            second = (column == SIDE * block + 7 - s).astype(bf16)
            mask_pos[pl.ds(s, tall, stride=SUB), :] = jnp.dot(
                picked, first, preferred_element_type=f32
            )
            mask_neg[pl.ds(s, tall, stride=SUB), :] = jnp.dot(
                picked, second, preferred_element_type=f32
            )

    def split(value):
        high = value.astype(bf16)
        return high, (value - high.astype(f32)).astype(bf16)

    def prepare_kernel():
        drift_kernel[...] = jnp.zeros_like(drift_kernel)
        for k in range(chunks):
            high, low = split(kern[k * LANES : (k + 1) * LANES, :])
            drift_kernel[k, 0:LANES, 0:drifts] = high
            drift_kernel[k, 0:LANES, LANES : LANES + drifts] = low
            drift_kernel[k, LANES : 2 * LANES, 0:drifts] = high

    def prepare_slots():
        down = lax.broadcasted_iota(i32, (held, held), 0)
        across = lax.broadcasted_iota(i32, (held, held), 1)
        owners = jnp.broadcast_to(owner[...].astype(f32), (held, held))
        owner_row = jnp.sum(jnp.where(down == across, owners, 0.0), axis=0, keepdims=True)
        earlier = (owners == owner_row) & (down < across)
        rank = jnp.sum(jnp.where(earlier, 1.0, 0.0), axis=0, keepdims=True)
        slot = owner_row * slots + rank
        for part in range(tiles * slots // LANES):
            at = lax.broadcasted_iota(i32, (LANES, held), 0) + part * LANES
            placer[part * LANES : (part + 1) * LANES, :] = (at.astype(f32) == slot).astype(bf16)
        wanted = jnp.broadcast_to(ocean[...].astype(f32) + 1.0, (held, held))
        target = jnp.sum(jnp.where(down == across, wanted, 0.0), axis=1, keepdims=True)
        lane = lax.broadcasted_iota(i32, (held, LANES), 1)
        stokes[...] = jnp.where(lane == drifts, target, jnp.where(lane == drifts + 1, 1.0, 0.0))

    def prepare_zeta():
        column = lax.broadcasted_iota(i32, (cols, cols), 1)

        def apart(first, second):
            one = (near[:, first : first + 1] == column).astype(f32)
            two = (near[:, second : second + 1] == column).astype(f32)
            return (one - two).astype(bf16)

        def taken(flow, picker):
            high, low = split(flow)
            rest = (flow - high.astype(f32) - low.astype(f32)).astype(bf16)
            total = jnp.zeros(flow.shape, f32)
            for each in (high, low, rest):
                total += lax.dot_general(
                    each, picker, (((1,), (1,)), ((), ())), preferred_element_type=f32
                )
            return total

        zeta[...] = taken(velocity[1], apart(0, 1)) - taken(velocity[0], apart(2, 3))

    def assemble(k):
        pos = jnp.broadcast_to(speed[1:2, lanes(k)] > 0.0, (rows, LANES))
        from_left = block > 0
        from_right = block < 63
        for s in range(SIDE):
            lower = jnp.where(from_left, left[k, s], 0.0)
            upper = jnp.where(from_right, right[k, SIDE - 1 - s], 0.0)
            wide[k, pl.ds(SIDE * SUB + s, rows, stride=SUB), :] = jnp.where(pos, lower, upper)
        for q in range(SIDE):
            wide[k, pl.ds(SIDE * SUB + SIDE + q, rows, stride=SUB), :] = jnp.where(
                pos, own[k, q], own[k, SIDE - 1 - q]
            )
        outside = pl.multiple_of((rows + SIDE) * SUB * grid, SUB)
        wide[k, pl.ds(outside, SIDE * SUB), :] = jnp.zeros((SIDE * SUB, LANES), f32)

    def sweep(k):
        spread = lambda v: jnp.broadcast_to(v, (SUB, LANES))
        cx = speed[0:1, lanes(k)]
        cy = speed[1:2, lanes(k)]
        down_rate = spread(jnp.maximum(cx, 0.0))
        up_rate = spread(jnp.maximum(-cx, 0.0))
        side_rate = spread(jnp.abs(cy))
        keep = 1.0 - down_rate - up_rate - side_rate
        pos = spread(cy) > 0.0

        @pl.loop(0, tall // SUB)
        def _(part):
            for u in range(SUB):
                at = pl.ds(pl.multiple_of((part * SUB + u) * SUB, SUB), SUB)
                mask_now[at, :] = jnp.where(pos, mask_pos[at, :], mask_neg[at, :])

        zero = jnp.zeros((SUB, LANES), f32)

        def part(i, carry):
            held_rows = [list(pair) for pair in carry[0]]
            masks = list(carry[1])
            for u in range(SUB):
                at = pl.ds(pl.multiple_of((i * SUB + u) * SUB, SUB), SUB)
                value = wide[k, at, :]
                for stage in range(SIDE):
                    previous, current = held_rows[stage]
                    moved = (
                        keep * current
                        + down_rate * previous
                        + up_rate * value
                        + side_rate * pltpu.roll(current, 1, 0)
                    )
                    held_rows[stage] = [current, value]
                    value = moved * masks[stage]
                swept[at, :] = value
                masks = [mask_now[at, :]] + masks[: SIDE - 1]
            return tuple(tuple(pair) for pair in held_rows), tuple(masks)

        start = (tuple((zero, zero) for _ in range(SIDE)), (zero,) * SIDE)
        lax.fori_loop(0, tall // SUB, part, start)
        wanted = jnp.broadcast_to(cy > 0.0, (rows, LANES))
        columns = [
            swept[pl.ds(2 * SIDE * SUB + SIDE + q, rows, stride=SUB), :] for q in range(SIDE)
        ]
        for c in range(SIDE):
            back[k, c] = jnp.where(wanted, columns[c], columns[SIDE - 1 - c])
        home[k, y] = back[k, y]
        for d in (2, 1, 3):
            send_out(k, d).start()

    def finish(k):
        for d in (1, 2, 3):
            send_out(k, d).wait_recv()
        for m in range(SIDE):
            final[k, pl.ds(m, rows, stride=SIDE), :] = home[k, m]
        store(k).start()
        both = jnp.concatenate(split(final[k]), axis=1)
        term = jnp.dot(both, drift_kernel[k], preferred_element_type=f32)
        stokes[...] += term[:, :LANES] + term[:, LANES:]

    relax(0)
    pl.semaphore_wait(barrier, tiles)
    launch(0)
    for k in (1, 2):
        relax(k)
        launch(k)

    @pl.loop(0, 3)
    def _(i):
        for each in range(2):
            relax(3 + 2 * i + each)
            launch(3 + 2 * i + each)
        forward(i)

    prepare_masks()

    @pl.loop(0, chunks)
    def _(t):
        @pl.when(t + 3 < chunks)
        def _():
            forward(t + 3)

        @pl.when(t == 0)
        def _():
            prepare_kernel()

        @pl.when(t == 1)
        def _():
            prepare_slots()

        @pl.when(t == 2)
        def _():
            prepare_zeta()

        for side in range(2):
            send_halo(t, side).wait_recv()
        assemble(t)
        send_edge(t).start()

        @pl.when(t >= 2)
        def _():
            finish(t - 2)

        send_edge(t).wait_recv()
        sweep(t)

    @pl.loop(chunks - 2, chunks)
    def _(k):
        finish(k)

    both = jnp.concatenate(split(stokes[...]), axis=1)
    per = tiles // 4
    for part in range(4):
        span = per * slots
        term = jnp.dot(
            placer[part * span : (part + 1) * span, :], both, preferred_element_type=f32
        )
        posted[part * per : (part + 1) * per] = (term[:, :LANES] + term[:, LANES:]).reshape(
            per, slots, LANES
        )

    @pl.loop(1, tiles)
    def _(d):
        post(d).start()

    arrived[place] = posted[place]

    @pl.loop(0, chunks)
    def _(k):
        for d in (1, 2, 3):
            send_in(k, d).wait_send()
            send_out(k, d).wait_send()
        for side in range(2):
            send_halo(k, side).wait_send()
        send_edge(k).wait_send()
        store(k).wait()

    def all_of(ref, sem):
        some = ref.at[pl.ds(0, tiles - 1)]
        return pltpu.make_async_copy(some, some, sem)

    all_of(arrived, post_recv).wait()
    rows_in = arrived[...].reshape(tiles * slots, LANES)
    target = rows_in[:, drifts : drifts + 1]
    column = lax.broadcasted_iota(i32, (tiles * slots, cols), 1).astype(f32) + 1.0
    chosen = (target == column).astype(bf16)
    summed = lax.dot_general(
        jnp.concatenate(split(rows_in), axis=1),
        chosen,
        (((0,), (0,)), ((), ())),
        preferred_element_type=f32,
    )
    summed = summed[:LANES] + summed[LANES:]
    count = jnp.maximum(summed[drifts + 1 : drifts + 2], 1.0)
    east_drift = summed[:levels] / count
    north_drift = summed[levels:drifts] / count
    spin = coriolis[...]
    turn = spin + zeta[...]
    east, north = velocity[0], velocity[1]
    velocity_out[0] = east + 0.25 * (spin * north + turn * north_drift)
    velocity_out[1] = north - 0.25 * (spin * east + turn * east_drift)
    all_of(posted, post_send).wait()


def per_device(
    spectrum,
    interaction,
    comp_speed,
    sea_mask,
    stokes_kernel,
    tile_owner,
    ocean_column,
    neighbours,
    coriolis,
    velocity,
):
    held, comps = spectrum.shape[1:]
    chunks = comps // LANES
    rows = held // SIDE
    tall = rows + 2 * SIDE
    tiles = lax.axis_size("pts")
    slots = 16
    levels, cols = velocity.shape[2:]
    f32, bf16 = jnp.float32, jnp.bfloat16
    piece = pltpu.VMEM((chunks, SIDE, rows, LANES), f32)
    mask = pltpu.VMEM((tall * SUB, LANES), f32)
    vmem = pl.BlockSpec(memory_space=pltpu.VMEM)
    anywhere = pl.BlockSpec(memory_space=pl.ANY)
    dma = pltpu.SemaphoreType.DMA
    spectrum_next, velocity_next = pl.pallas_call(
        wave_kernel,
        out_shape=(
            jax.ShapeDtypeStruct((held, comps), f32),
            jax.ShapeDtypeStruct((2, levels, cols), f32),
        ),
        in_specs=[anywhere, anywhere] + [vmem] * 8,
        out_specs=(anywhere, vmem),
        scratch_shapes=[
            pltpu.VMEM((chunks, held, LANES), f32),
            pltpu.VMEM((chunks, comps, LANES), bf16),
            pltpu.VMEM((held, comps), bf16),
            piece,
            piece,
            piece,
            piece,
            pltpu.VMEM((chunks, tall * SUB, LANES), f32),
            mask,
            piece,
            piece,
            pltpu.VMEM((chunks, held, LANES), f32),
            mask,
            mask,
            mask,
            pltpu.VMEM((2 * rows, GC), f32),
            pltpu.VMEM((chunks, 2 * LANES, 2 * LANES), bf16),
            pltpu.VMEM((held, LANES), f32),
            pltpu.VMEM((tiles * slots, held), bf16),
            pltpu.VMEM((levels, cols), f32),
            pltpu.VMEM((tiles, slots, LANES), f32),
            pltpu.VMEM((tiles, slots, LANES), f32),
            dma((2, chunks)),
            dma((chunks,)),
            dma((chunks, 3)),
            dma((chunks, 3)),
            dma((chunks, 2)),
            dma((chunks, 2)),
            dma((chunks,)),
            dma((chunks,)),
            dma((chunks, 3)),
            dma((chunks, 3)),
            dma(()),
            dma(()),
        ],
        compiler_params=pltpu.CompilerParams(
            collective_id=0, has_side_effects=True, vmem_limit_bytes=56 << 20
        ),
        name="wave_step",
    )(
        spectrum[0],
        interaction,
        comp_speed,
        sea_mask,
        stokes_kernel,
        tile_owner[0],
        ocean_column,
        neighbours[0],
        coriolis,
        velocity[0],
    )
    return (spectrum_next[None], velocity_next[None])


def solution(mesh):
    placed = (
        P("grid", "pts", None),
        P(),
        P(),
        P(),
        P(),
        P("grid", "pts", None),
        P("grid", "pts"),
        P("grid", "pts", None),
        P("grid", "pts"),
        P("grid", None, None, "pts"),
    )
    return jax.shard_map(
        per_device,
        mesh=mesh,
        in_specs=placed,
        out_specs=(P("grid", "pts", None), P("grid", None, None, "pts")),
        check_vma=False,
    )
```

```python
import jax
import jax.numpy as jnp
from jax import lax
from jax.experimental import pallas as pl
from jax.experimental.pallas import tpu as pltpu
from jax.sharding import PartitionSpec as P

MESH = pl.DeviceIdType.MESH
LANES = 128
SUB = 8
SIDE = 4
GC = 256


def wave_kernel(
    spec_hbm,
    inter_hbm,
    speed,
    sea,
    kern,
    owner,
    ocean,
    near,
    coriolis,
    velocity,
    out_hbm,
    velocity_out,
    spec,
    inter,
    half,
    sent,
    own,
    left,
    right,
    wide,
    swept,
    back,
    home,
    final,
    mask_pos,
    mask_neg,
    mask_now,
    sea_rows,
    drift_kernel,
    stokes,
    placer,
    zeta,
    posted,
    arrived,
    load_sem,
    store_sem,
    in_send,
    in_recv,
    halo_send,
    halo_recv,
    edge_send,
    edge_recv,
    out_send,
    out_recv,
    post_send,
    post_recv,
):
    f32, bf16, i32 = jnp.float32, jnp.bfloat16, jnp.int32
    chunks, held = spec.shape[:2]
    rows = held // SIDE
    tall = rows + 2 * SIDE
    tiles, slots = arrived.shape[:2]
    drifts = kern.shape[0]
    levels = drifts // 2
    cols = coriolis.shape[1]
    grid = lax.axis_index("grid")
    place = lax.axis_index("pts")
    y = lax.rem(place, SIDE)
    base = place - y
    rings = tiles // SIDE
    ring = place // SIDE
    peers = [base + lax.rem(y + d, SIDE) for d in (1, 2, 3)]
    lanes = lambda k: pl.ds(pl.multiple_of(k * LANES, LANES), LANES)

    def turned(k, r):
        return (r - (k + k // 3) + rings - 1) // rings

    def group(k):
        return lax.rem(y - turned(k, ring) + SIDE, SIDE)

    def block(k):
        return rings * group(k) + ring

    def beside(k, step):
        other = lax.rem(ring + step + rings, rings)
        across = (ring + step + rings) // rings - 1
        turn = across + turned(k, other) - turned(k, ring)
        return SIDE * other + lax.rem(y + turn + 2 * SIDE, SIDE)

    def load_spec(k):
        return pltpu.make_async_copy(spec_hbm.at[:, lanes(k)], spec.at[k], load_sem.at[0, k])

    def load_inter(k):
        return pltpu.make_async_copy(inter_hbm.at[:, lanes(k)], inter.at[k], load_sem.at[1, k])

    barrier = pltpu.get_barrier_semaphore()

    @pl.loop(1, tiles)
    def _(d):
        pl.semaphore_signal(
            barrier, inc=1, device_id={"pts": lax.rem(place + d, tiles)}, device_id_type=MESH
        )

    pl.semaphore_signal(barrier, inc=1, device_id={"grid": 1 - grid}, device_id_type=MESH)

    @pl.loop(0, chunks)
    def _(k):
        load_spec(k).start()

    @pl.loop(0, chunks)
    def _(k):
        load_inter(k).start()

    for k in range(chunks):
        load_spec(k).wait()
        for m in range(SIDE):
            half[m * rows : (m + 1) * rows, k * LANES : (k + 1) * LANES] = spec[
                k, pl.ds(m, rows, stride=SIDE), :
            ].astype(bf16)

    def send_in(k, d):
        return pltpu.make_async_remote_copy(
            src_ref=sent.at[k, lax.rem(group(k) + d, SIDE)],
            dst_ref=own.at[k, y],
            send_sem=in_send.at[k, d - 1],
            recv_sem=in_recv.at[k, d - 1],
            device_id={"pts": peers[d - 1]},
            device_id_type=MESH,
        )

    def send_halo(k, side):
        return pltpu.make_async_remote_copy(
            src_ref=own.at[k],
            dst_ref=(left if side == 0 else right).at[k],
            send_sem=halo_send.at[k, side],
            recv_sem=halo_recv.at[k, side],
            device_id={"pts": beside(k, 1 if side == 0 else -1)},
            device_id_type=MESH,
        )

    def send_edge(k):
        at = pl.multiple_of((rows - (rows - SIDE) * grid) * SUB, SUB)
        to = pl.multiple_of((rows + SIDE) * SUB * grid, SUB)
        return pltpu.make_async_remote_copy(
            src_ref=wide.at[k, pl.ds(at, SIDE * SUB)],
            dst_ref=wide.at[k, pl.ds(to, SIDE * SUB)],
            send_sem=edge_send.at[k],
            recv_sem=edge_recv.at[k],
            device_id={"grid": 1 - grid},
            device_id_type=MESH,
        )

    def send_out(k, d):
        return pltpu.make_async_remote_copy(
            src_ref=back.at[k, lax.rem(y + d, SIDE)],
            dst_ref=home.at[k, group(k)],
            send_sem=out_send.at[k, d - 1],
            recv_sem=out_recv.at[k, d - 1],
            device_id={"pts": peers[d - 1]},
            device_id_type=MESH,
        )

    def post(d):
        peer = lax.rem(place + d, tiles)
        return pltpu.make_async_remote_copy(
            src_ref=posted.at[peer],
            dst_ref=arrived.at[place],
            send_sem=post_send,
            recv_sem=post_recv,
            device_id={"pts": peer},
            device_id_type=MESH,
        )

    def store(k):
        return pltpu.make_async_copy(final.at[k], out_hbm.at[:, lanes(k)], store_sem.at[k])

    def relax(k):
        load_inter(k).wait()
        mix = jnp.dot(half[...], inter[k], preferred_element_type=f32)
        grown = jnp.tanh(mix)
        for m in range(SIDE):
            local = spec[k, pl.ds(m, rows, stride=SIDE), :]
            sent[k, m] = local + 0.5 * local * grown[m * rows : (m + 1) * rows]
        own[k, y] = sent[k, group(k)]

    def launch(k):
        for d in (2, 1, 3):
            send_in(k, d).start()

    def forward(k):
        for d in (1, 2, 3):
            send_in(k, d).wait_recv()
        for side in range(2):
            send_halo(k, side).start()

    def prepare_masks():
        @pl.loop(0, rows)
        def _(r):
            pair = sea[:, pl.ds(pl.multiple_of(r * GC, GC), GC)].astype(f32)
            sea_rows[pl.ds(r, 1), :] = pair[0:1]
            sea_rows[pl.ds(r + rows, 1), :] = pair[1:2]

        row_at = lax.broadcasted_iota(i32, (tall, 2 * rows), 0) + (rows * grid - SIDE)
        row_of = lax.broadcasted_iota(i32, (tall, 2 * rows), 1)
        picked = jnp.dot(
            (row_at == row_of).astype(bf16),
            sea_rows[...].astype(bf16),
            preferred_element_type=f32,
        ).astype(bf16)
        column = lax.broadcasted_iota(i32, (GC, LANES), 0)
        for turn in range(2):
            start = SIDE * (rings * lax.rem(y - turn + SIDE, SIDE) + ring)
            for s in range(SUB):
                first = (column == start - SIDE + s).astype(bf16)
                second = (column == start + 7 - s).astype(bf16)
                mask_pos[turn, pl.ds(s, tall, stride=SUB), :] = jnp.dot(
                    picked, first, preferred_element_type=f32
                )
                mask_neg[turn, pl.ds(s, tall, stride=SUB), :] = jnp.dot(
                    picked, second, preferred_element_type=f32
                )

    def split(value):
        high = value.astype(bf16)
        return high, (value - high.astype(f32)).astype(bf16)

    def prepare_kernel():
        drift_kernel[...] = jnp.zeros_like(drift_kernel)
        for k in range(chunks):
            high, low = split(kern[:, k * LANES : (k + 1) * LANES])
            drift_kernel[k, 0:drifts, 0:LANES] = high
            drift_kernel[k, 0:drifts, LANES : 2 * LANES] = high
            drift_kernel[k, LANES : LANES + drifts, 0:LANES] = low

    def prepare_slots():
        down = lax.broadcasted_iota(i32, (held, held), 0)
        across = lax.broadcasted_iota(i32, (held, held), 1)
        owner_row = owner[...].astype(f32)
        owners = jnp.broadcast_to(owner_row, (held, held))
        owner_column = jnp.sum(jnp.where(down == across, owners, 0.0), axis=1, keepdims=True)
        earlier = (owners == owner_column) & (down < across)
        rank = jnp.sum(jnp.where(earlier, 1.0, 0.0), axis=0, keepdims=True)
        slot = owner_row * slots + rank
        for part in range(tiles * slots // LANES):
            at = lax.broadcasted_iota(i32, (LANES, held), 0) + part * LANES
            placer[part * LANES : (part + 1) * LANES, :] = (at.astype(f32) == slot).astype(bf16)
        wanted = jnp.broadcast_to(ocean[...].astype(f32) + 1.0, (held, held))
        target = jnp.sum(jnp.where(down == across, wanted, 0.0), axis=1, keepdims=True)
        lane = lax.broadcasted_iota(i32, (held, LANES), 1)
        stokes[...] = jnp.where(lane == drifts, target, jnp.where(lane == drifts + 1, 1.0, 0.0))

    def prepare_zeta():
        column = lax.broadcasted_iota(i32, (cols, cols), 0)

        def apart(first, second):
            one = (near[first : first + 1, :] == column).astype(f32)
            two = (near[second : second + 1, :] == column).astype(f32)
            return (one - two).astype(bf16)

        def taken(flow, picker):
            high, low = split(flow)
            rest = (flow - high.astype(f32) - low.astype(f32)).astype(bf16)
            total = jnp.zeros(flow.shape, f32)
            for each in (high, low, rest):
                total += jnp.dot(each, picker, preferred_element_type=f32)
            return total

        zeta[...] = taken(velocity[1], apart(0, 1)) - taken(velocity[0], apart(2, 3))

    def assemble(k):
        pos = jnp.broadcast_to(speed[1:2, lanes(k)] > 0.0, (rows, LANES))
        from_left = block(k) > 0
        from_right = block(k) < tiles - 1
        for s in range(SIDE):
            lower = jnp.where(from_left, left[k, s], 0.0)
            upper = jnp.where(from_right, right[k, SIDE - 1 - s], 0.0)
            wide[k, pl.ds(SIDE * SUB + s, rows, stride=SUB), :] = jnp.where(pos, lower, upper)
        for q in range(SIDE):
            wide[k, pl.ds(SIDE * SUB + SIDE + q, rows, stride=SUB), :] = jnp.where(
                pos, own[k, q], own[k, SIDE - 1 - q]
            )
        outside = pl.multiple_of((rows + SIDE) * SUB * grid, SUB)
        wide[k, pl.ds(outside, SIDE * SUB), :] = jnp.zeros((SIDE * SUB, LANES), f32)

    def sweep(k):
        spread = lambda v: jnp.broadcast_to(v, (SUB, LANES))
        cx = speed[0:1, lanes(k)]
        cy = speed[1:2, lanes(k)]
        down_rate = spread(jnp.maximum(cx, 0.0))
        up_rate = spread(jnp.maximum(-cx, 0.0))
        side_rate = spread(jnp.abs(cy))
        keep = 1.0 - down_rate - up_rate - side_rate
        pos = spread(cy) > 0.0
        turn = turned(k, ring)

        @pl.loop(0, tall // SUB)
        def _(part):
            for u in range(SUB):
                at = pl.ds(pl.multiple_of((part * SUB + u) * SUB, SUB), SUB)
                mask_now[at, :] = jnp.where(pos, mask_pos[turn, at, :], mask_neg[turn, at, :])

        zero = jnp.zeros((SUB, LANES), f32)

        def part(i, carry):
            held_rows = [list(pair) for pair in carry[0]]
            masks = list(carry[1])
            for u in range(SUB):
                at = pl.ds(pl.multiple_of((i * SUB + u) * SUB, SUB), SUB)
                value = wide[k, at, :]
                for stage in range(SIDE):
                    previous, current = held_rows[stage]
                    moved = (
                        keep * current
                        + down_rate * previous
                        + up_rate * value
                        + side_rate * pltpu.roll(current, 1, 0)
                    )
                    held_rows[stage] = [current, value]
                    value = moved * masks[stage]
                swept[at, :] = value
                masks = [mask_now[at, :]] + masks[: SIDE - 1]
            return tuple(tuple(pair) for pair in held_rows), tuple(masks)

        start = (tuple((zero, zero) for _ in range(SIDE)), (zero,) * SIDE)
        lax.fori_loop(0, tall // SUB, part, start)
        wanted = jnp.broadcast_to(cy > 0.0, (rows, LANES))
        columns = [
            swept[pl.ds(2 * SIDE * SUB + SIDE + q, rows, stride=SUB), :] for q in range(SIDE)
        ]
        for c in range(SIDE):
            back[k, c] = jnp.where(wanted, columns[c], columns[SIDE - 1 - c])
        home[k, group(k)] = back[k, y]
        for d in (2, 1, 3):
            send_out(k, d).start()

    def finish(k):
        for d in (1, 2, 3):
            send_out(k, d).wait_recv()
        for m in range(SIDE):
            final[k, pl.ds(m, rows, stride=SIDE), :] = home[k, m]
        store(k).start()
        both = jnp.concatenate(split(final[k]), axis=1)
        term = lax.dot_general(
            both, drift_kernel[k], (((1,), (1,)), ((), ())), preferred_element_type=f32
        )
        stokes[...] += term[:, :LANES] + term[:, LANES:]

    relax(0)
    pl.semaphore_wait(barrier, tiles)
    launch(0)
    for k in (1, 2):
        relax(k)
        launch(k)

    @pl.loop(0, 3)
    def _(i):
        for each in range(2):
            relax(3 + 2 * i + each)
            launch(3 + 2 * i + each)
        forward(i)

    prepare_masks()

    @pl.loop(0, chunks)
    def _(t):
        @pl.when(t + 3 < chunks)
        def _():
            forward(t + 3)

        @pl.when(t == 0)
        def _():
            prepare_kernel()

        @pl.when(t == 1)
        def _():
            prepare_slots()

        @pl.when(t == 2)
        def _():
            prepare_zeta()

        for side in range(2):
            send_halo(t, side).wait_recv()
        assemble(t)
        send_edge(t).start()

        @pl.when(t >= 2)
        def _():
            finish(t - 2)

        send_edge(t).wait_recv()
        sweep(t)

    @pl.loop(chunks - 2, chunks)
    def _(k):
        finish(k)

    both = jnp.concatenate(split(stokes[...]), axis=1)
    per = tiles // 4
    for part in range(4):
        span = per * slots
        term = jnp.dot(
            placer[part * span : (part + 1) * span, :], both, preferred_element_type=f32
        )
        posted[part * per : (part + 1) * per] = (term[:, :LANES] + term[:, LANES:]).reshape(
            per, slots, LANES
        )

    @pl.loop(1, tiles)
    def _(d):
        post(d).start()

    arrived[place] = posted[place]

    @pl.loop(0, chunks)
    def _(k):
        for d in (1, 2, 3):
            send_in(k, d).wait_send()
            send_out(k, d).wait_send()
        for side in range(2):
            send_halo(k, side).wait_send()
        send_edge(k).wait_send()
        store(k).wait()

    def all_of(ref, sem):
        some = ref.at[pl.ds(0, tiles - 1)]
        return pltpu.make_async_copy(some, some, sem)

    all_of(arrived, post_recv).wait()
    rows_in = arrived[...].reshape(tiles * slots, LANES)
    target = rows_in[:, drifts : drifts + 1]
    column = lax.broadcasted_iota(i32, (tiles * slots, cols), 1).astype(f32) + 1.0
    chosen = (target == column).astype(bf16)
    summed = lax.dot_general(
        jnp.concatenate(split(rows_in), axis=1),
        chosen,
        (((0,), (0,)), ((), ())),
        preferred_element_type=f32,
    )
    summed = summed[:LANES] + summed[LANES:]
    count = jnp.maximum(summed[drifts + 1 : drifts + 2], 1.0)
    east_drift = summed[:levels] / count
    north_drift = summed[levels:drifts] / count
    spin = coriolis[...]
    turn = spin + zeta[...]
    east, north = velocity[0], velocity[1]
    velocity_out[0] = east + 0.25 * (spin * north + turn * north_drift)
    velocity_out[1] = north - 0.25 * (spin * east + turn * east_drift)
    all_of(posted, post_send).wait()


def per_device(
    spectrum,
    interaction,
    comp_speed,
    sea_mask,
    stokes_kernel,
    tile_owner,
    ocean_column,
    neighbours,
    coriolis,
    velocity,
):
    held, comps = spectrum.shape[1:]
    chunks = comps // LANES
    rows = held // SIDE
    tall = rows + 2 * SIDE
    tiles = lax.axis_size("pts")
    slots = 16
    levels, cols = velocity.shape[2:]
    f32, bf16 = jnp.float32, jnp.bfloat16
    piece = pltpu.VMEM((chunks, SIDE, rows, LANES), f32)
    mask = pltpu.VMEM((tall * SUB, LANES), f32)
    vmem = pl.BlockSpec(memory_space=pltpu.VMEM)
    anywhere = pl.BlockSpec(memory_space=pl.ANY)
    dma = pltpu.SemaphoreType.DMA
    spectrum_next, velocity_next = pl.pallas_call(
        wave_kernel,
        out_shape=(
            jax.ShapeDtypeStruct((held, comps), f32),
            jax.ShapeDtypeStruct((2, levels, cols), f32),
        ),
        in_specs=[anywhere, anywhere] + [vmem] * 8,
        out_specs=(anywhere, vmem),
        scratch_shapes=[
            pltpu.VMEM((chunks, held, LANES), f32),
            pltpu.VMEM((chunks, comps, LANES), bf16),
            pltpu.VMEM((held, comps), bf16),
            piece,
            piece,
            piece,
            piece,
            pltpu.VMEM((chunks, tall * SUB, LANES), f32),
            mask,
            piece,
            piece,
            pltpu.VMEM((chunks, held, LANES), f32),
            pltpu.VMEM((2, tall * SUB, LANES), f32),
            pltpu.VMEM((2, tall * SUB, LANES), f32),
            mask,
            pltpu.VMEM((2 * rows, GC), f32),
            pltpu.VMEM((chunks, 2 * LANES, 2 * LANES), bf16),
            pltpu.VMEM((held, LANES), f32),
            pltpu.VMEM((tiles * slots, held), bf16),
            pltpu.VMEM((levels, cols), f32),
            pltpu.VMEM((tiles, slots, LANES), f32),
            pltpu.VMEM((tiles, slots, LANES), f32),
            dma((2, chunks)),
            dma((chunks,)),
            dma((chunks, 3)),
            dma((chunks, 3)),
            dma((chunks, 2)),
            dma((chunks, 2)),
            dma((chunks,)),
            dma((chunks,)),
            dma((chunks, 3)),
            dma((chunks, 3)),
            dma(()),
            dma(()),
        ],
        compiler_params=pltpu.CompilerParams(
            collective_id=0, has_side_effects=True, vmem_limit_bytes=56 << 20
        ),
        name="wave_step",
    )(
        spectrum[0],
        interaction,
        comp_speed,
        sea_mask,
        stokes_kernel.T,
        tile_owner.reshape(1, held),
        ocean_column,
        neighbours[0].T,
        coriolis,
        velocity[0],
    )
    return (spectrum_next[None], velocity_next[None])


def solution(mesh):
    placed = (
        P("grid", "pts", None),
        P(),
        P(),
        P(),
        P(),
        P("grid", "pts", None),
        P("grid", "pts"),
        P("grid", "pts", None),
        P("grid", "pts"),
        P("grid", None, None, "pts"),
    )
    return jax.shard_map(
        per_device,
        mesh=mesh,
        in_specs=placed,
        out_specs=(P("grid", "pts", None), P("grid", None, None, "pts")),
        check_vma=False,
    )
```

```python
import jax
import jax.numpy as jnp
from jax import lax
from jax.experimental import pallas as pl
from jax.experimental.pallas import tpu as pltpu
from jax.sharding import PartitionSpec as P

MESH = pl.DeviceIdType.MESH
LANES = 128
SUB = 8
SIDE = 4
GC = 256


def wave_kernel(
    spec_hbm,
    inter_hbm,
    sea_hbm,
    kern_hbm,
    velocity_hbm,
    speed_hbm,
    owner_hbm,
    ocean_hbm,
    near_hbm,
    out_hbm,
    arrived_out,
    zeta,
    sea,
    kern,
    velocity,
    speed,
    owner,
    ocean,
    near,
    spec,
    inter,
    half,
    sent,
    own,
    left,
    right,
    wide,
    swept,
    back,
    home,
    final,
    mask_pos,
    mask_neg,
    mask_now,
    sea_rows,
    drift_kernel,
    stokes,
    placer,
    posted,
    arrived,
    load_sem,
    side_sem,
    store_sem,
    in_send,
    in_recv,
    halo_send,
    halo_recv,
    edge_send,
    edge_recv,
    out_send,
    out_recv,
    post_send,
    post_recv,
    first_send,
    first_recv,
):
    f32, bf16, i32 = jnp.float32, jnp.bfloat16, jnp.int32
    chunks, held = spec.shape[:2]
    rows = held // SIDE
    tall = rows + 2 * SIDE
    tiles, slots = arrived.shape[:2]
    drifts = kern.shape[0]
    cols = near.shape[1]
    grid = lax.axis_index("grid")
    place = lax.axis_index("pts")
    y = lax.rem(place, SIDE)
    base = place - y
    rings = tiles // SIDE
    ring = place // SIDE
    peers = [base + lax.rem(y + d, SIDE) for d in (1, 2, 3)]
    lanes = lambda k: pl.ds(pl.multiple_of(k * LANES, LANES), LANES)

    def turned(k, r):
        return (r - (k + k // 3) + rings - 1) // rings

    def group(k):
        return lax.rem(y - turned(k, ring) + SIDE, SIDE)

    def block(k):
        return rings * group(k) + ring

    def beside(k, step):
        other = lax.rem(ring + step + rings, rings)
        across = (ring + step + rings) // rings - 1
        turn = across + turned(k, other) - turned(k, ring)
        return SIDE * other + lax.rem(y + turn + 2 * SIDE, SIDE)

    def load_spec(k):
        return pltpu.make_async_copy(spec_hbm.at[:, lanes(k)], spec.at[k], load_sem.at[0, k])

    def load_inter(k):
        return pltpu.make_async_copy(inter_hbm.at[:, lanes(k)], inter.at[k], load_sem.at[1, k])

    barrier = pltpu.get_barrier_semaphore()

    @pl.loop(1, tiles)
    def _(d):
        pl.semaphore_signal(
            barrier, inc=1, device_id={"pts": lax.rem(place + d, tiles)}, device_id_type=MESH
        )

    pl.semaphore_signal(barrier, inc=1, device_id={"grid": 1 - grid}, device_id_type=MESH)

    @pl.loop(0, chunks)
    def _(k):
        load_spec(k).start()

    @pl.loop(0, chunks)
    def _(k):
        load_inter(k).start()

    side_loads = [
        pltpu.make_async_copy(source, target, side_sem.at[i])
        for i, (source, target) in enumerate(
            [
                (sea_hbm, sea),
                (kern_hbm, kern),
                (velocity_hbm, velocity),
                (speed_hbm, speed),
                (owner_hbm, owner),
                (ocean_hbm, ocean),
                (near_hbm, near),
            ]
        )
    ]
    for each in side_loads:
        each.start()

    for k in range(chunks):
        load_spec(k).wait()
        for m in range(SIDE):
            half[m * rows : (m + 1) * rows, k * LANES : (k + 1) * LANES] = spec[
                k, pl.ds(m, rows, stride=SIDE), :
            ].astype(bf16)

    def send_in(k, d):
        return pltpu.make_async_remote_copy(
            src_ref=sent.at[k, lax.rem(group(k) + d, SIDE)],
            dst_ref=own.at[k, y],
            send_sem=in_send.at[k, d - 1],
            recv_sem=in_recv.at[k, d - 1],
            device_id={"pts": peers[d - 1]},
            device_id_type=MESH,
        )

    def send_halo(k, side):
        return pltpu.make_async_remote_copy(
            src_ref=own.at[k],
            dst_ref=(left if side == 0 else right).at[k],
            send_sem=halo_send.at[k, side],
            recv_sem=halo_recv.at[k, side],
            device_id={"pts": beside(k, 1 if side == 0 else -1)},
            device_id_type=MESH,
        )

    def send_first(c, side):
        return pltpu.make_async_remote_copy(
            src_ref=own.at[0, c],
            dst_ref=(left if side == 0 else right).at[0, c],
            send_sem=first_send.at[c, side],
            recv_sem=first_recv.at[c, side],
            device_id={"pts": beside(0, 1 if side == 0 else -1)},
            device_id_type=MESH,
        )

    def send_edge(k):
        at = pl.multiple_of((rows - (rows - SIDE) * grid) * SUB, SUB)
        to = pl.multiple_of((rows + SIDE) * SUB * grid, SUB)
        return pltpu.make_async_remote_copy(
            src_ref=wide.at[k, pl.ds(at, SIDE * SUB)],
            dst_ref=wide.at[k, pl.ds(to, SIDE * SUB)],
            send_sem=edge_send.at[k],
            recv_sem=edge_recv.at[k],
            device_id={"grid": 1 - grid},
            device_id_type=MESH,
        )

    def send_out(k, d):
        return pltpu.make_async_remote_copy(
            src_ref=back.at[k, lax.rem(y + d, SIDE)],
            dst_ref=home.at[k, group(k)],
            send_sem=out_send.at[k, d - 1],
            recv_sem=out_recv.at[k, d - 1],
            device_id={"pts": peers[d - 1]},
            device_id_type=MESH,
        )

    def post(peer):
        return pltpu.make_async_remote_copy(
            src_ref=posted.at[peer],
            dst_ref=arrived.at[place],
            send_sem=post_send,
            recv_sem=post_recv,
            device_id={"pts": peer},
            device_id_type=MESH,
        )

    def store(k):
        return pltpu.make_async_copy(final.at[k], out_hbm.at[:, lanes(k)], store_sem.at[k])

    def relax(k):
        load_inter(k).wait()
        mix = jnp.dot(half[...], inter[k], preferred_element_type=f32)
        grown = jnp.tanh(mix)
        for m in range(SIDE):
            local = spec[k, pl.ds(m, rows, stride=SIDE), :]
            sent[k, m] = local + 0.5 * local * grown[m * rows : (m + 1) * rows]
        own[k, y] = sent[k, group(k)]

    def launch(k):
        for d in (2, 1, 3):
            send_in(k, d).start()

    def forward(k):
        for d in (1, 2, 3):
            send_in(k, d).wait_recv()
        for side in range(2):
            send_halo(k, side).start()

    def prepare_masks():
        @pl.loop(0, rows)
        def _(r):
            pair = sea[:, pl.ds(pl.multiple_of(r * GC, GC), GC)].astype(f32)
            sea_rows[pl.ds(r, 1), :] = pair[0:1]
            sea_rows[pl.ds(r + rows, 1), :] = pair[1:2]

        row_at = lax.broadcasted_iota(i32, (tall, 2 * rows), 0) + (rows * grid - SIDE)
        row_of = lax.broadcasted_iota(i32, (tall, 2 * rows), 1)
        picked = jnp.dot(
            (row_at == row_of).astype(bf16),
            sea_rows[...].astype(bf16),
            preferred_element_type=f32,
        ).astype(bf16)
        column = lax.broadcasted_iota(i32, (GC, LANES), 0)
        for turn in range(2):
            start = SIDE * (rings * lax.rem(y - turn + SIDE, SIDE) + ring)
            for s in range(SUB):
                first = (column == start - SIDE + s).astype(bf16)
                second = (column == start + 7 - s).astype(bf16)
                mask_pos[turn, pl.ds(s, tall, stride=SUB), :] = jnp.dot(
                    picked, first, preferred_element_type=f32
                )
                mask_neg[turn, pl.ds(s, tall, stride=SUB), :] = jnp.dot(
                    picked, second, preferred_element_type=f32
                )

    def prepare_kernel():
        drift_kernel[...] = jnp.zeros_like(drift_kernel)
        for k in range(chunks):
            high, low = split(kern[:, k * LANES : (k + 1) * LANES])
            drift_kernel[k, 0:drifts, 0:LANES] = high
            drift_kernel[k, 0:drifts, LANES : 2 * LANES] = high
            drift_kernel[k, LANES : LANES + drifts, 0:LANES] = low

    def prepare_slots():
        down = lax.broadcasted_iota(i32, (held, held), 0)
        across = lax.broadcasted_iota(i32, (held, held), 1)
        owner_row = owner[...].astype(f32)
        owners = jnp.broadcast_to(owner_row, (held, held))
        owner_column = jnp.sum(jnp.where(down == across, owners, 0.0), axis=1, keepdims=True)
        earlier = (owners == owner_column) & (down < across)
        rank = jnp.sum(jnp.where(earlier, 1.0, 0.0), axis=0, keepdims=True)
        slot = owner_row * slots + rank
        for part in range(tiles * slots // LANES):
            at = lax.broadcasted_iota(i32, (LANES, held), 0) + part * LANES
            placer[part * LANES : (part + 1) * LANES, :] = (at.astype(f32) == slot).astype(bf16)
        wanted = jnp.broadcast_to(ocean[...].astype(f32) + 1.0, (held, held))
        target = jnp.sum(jnp.where(down == across, wanted, 0.0), axis=1, keepdims=True)
        lane = lax.broadcasted_iota(i32, (held, LANES), 1)
        stokes[...] = jnp.where(lane == drifts, target, jnp.where(lane == drifts + 1, 1.0, 0.0))

    def prepare_zeta():
        column = lax.broadcasted_iota(i32, (cols, cols), 0)

        def apart(first, second):
            one = (near[first : first + 1, :] == column).astype(f32)
            two = (near[second : second + 1, :] == column).astype(f32)
            return (one - two).astype(bf16)

        def taken(flow, picker):
            high, low = split(flow)
            rest = (flow - high.astype(f32) - low.astype(f32)).astype(bf16)
            total = jnp.zeros(flow.shape, f32)
            for each in (high, low, rest):
                total += jnp.dot(each, picker, preferred_element_type=f32)
            return total

        zeta[...] = taken(velocity[1], apart(0, 1)) - taken(velocity[0], apart(2, 3))

    def assemble(k):
        pos = jnp.broadcast_to(speed[1:2, lanes(k)] > 0.0, (rows, LANES))
        from_left = block(k) > 0
        from_right = block(k) < tiles - 1
        for s in range(SIDE):
            lower = jnp.where(from_left, left[k, s], 0.0)
            upper = jnp.where(from_right, right[k, SIDE - 1 - s], 0.0)
            wide[k, pl.ds(SIDE * SUB + s, rows, stride=SUB), :] = jnp.where(pos, lower, upper)
        for q in range(SIDE):
            wide[k, pl.ds(SIDE * SUB + SIDE + q, rows, stride=SUB), :] = jnp.where(
                pos, own[k, q], own[k, SIDE - 1 - q]
            )
        outside = pl.multiple_of((rows + SIDE) * SUB * grid, SUB)
        wide[k, pl.ds(outside, SIDE * SUB), :] = jnp.zeros((SIDE * SUB, LANES), f32)

    def sweep(k):
        spread = lambda v: jnp.broadcast_to(v, (SUB, LANES))
        cx = speed[0:1, lanes(k)]
        cy = speed[1:2, lanes(k)]
        down_rate = spread(jnp.maximum(cx, 0.0))
        up_rate = spread(jnp.maximum(-cx, 0.0))
        side_rate = spread(jnp.abs(cy))
        keep = 1.0 - down_rate - up_rate - side_rate
        pos = spread(cy) > 0.0
        turn = turned(k, ring)

        @pl.loop(0, tall // SUB)
        def _(part):
            for u in range(SUB):
                at = pl.ds(pl.multiple_of((part * SUB + u) * SUB, SUB), SUB)
                mask_now[at, :] = jnp.where(pos, mask_pos[turn, at, :], mask_neg[turn, at, :])

        zero = jnp.zeros((SUB, LANES), f32)

        def part(i, carry):
            held_rows = [list(pair) for pair in carry[0]]
            masks = list(carry[1])
            for u in range(SUB):
                at = pl.ds(pl.multiple_of((i * SUB + u) * SUB, SUB), SUB)
                value = wide[k, at, :]
                for stage in range(SIDE):
                    previous, current = held_rows[stage]
                    moved = (
                        keep * current
                        + down_rate * previous
                        + up_rate * value
                        + side_rate * pltpu.roll(current, 1, 0)
                    )
                    held_rows[stage] = [current, value]
                    value = moved * masks[stage]
                swept[at, :] = value
                masks = [mask_now[at, :]] + masks[: SIDE - 1]
            return tuple(tuple(pair) for pair in held_rows), tuple(masks)

        start = (tuple((zero, zero) for _ in range(SIDE)), (zero,) * SIDE)
        lax.fori_loop(0, tall // SUB, part, start)
        wanted = jnp.broadcast_to(cy > 0.0, (rows, LANES))
        columns = [
            swept[pl.ds(2 * SIDE * SUB + SIDE + q, rows, stride=SUB), :] for q in range(SIDE)
        ]
        for c in range(SIDE):
            back[k, c] = jnp.where(wanted, columns[c], columns[SIDE - 1 - c])
        home[k, group(k)] = back[k, y]
        for d in (2, 1, 3):
            send_out(k, d).start()

    def finish(k):
        for d in (1, 2, 3):
            send_out(k, d).wait_recv()
        for m in range(SIDE):
            final[k, pl.ds(m, rows, stride=SIDE), :] = home[k, m]
        store(k).start()
        both = jnp.concatenate(split(final[k]), axis=1)
        term = lax.dot_general(
            both, drift_kernel[k], (((1,), (1,)), ((), ())), preferred_element_type=f32
        )
        stokes[...] += term[:, :LANES] + term[:, LANES:]

    relax(0)
    pl.semaphore_wait(barrier, tiles)
    launch(0)
    for side in range(2):
        send_first(y, side).start()
    for k in (1, 2):
        relax(k)
        launch(k)
    for d in (1, 3, 2):
        send_in(0, d).wait_recv()
        for side in range(2):
            send_first(lax.rem(y - d + SIDE, SIDE), side).start()

    @pl.loop(1, 3)
    def _(i):
        for each in range(3):
            relax(3 * i + each)
            launch(3 * i + each)
        forward(i)

    for each in side_loads:
        each.wait()
    prepare_masks()

    @pl.loop(0, chunks)
    def _(t):
        @pl.when(t + 3 < chunks)
        def _():
            forward(t + 3)

        @pl.when(t == 0)
        def _():
            prepare_kernel()

        @pl.when(t == 1)
        def _():
            prepare_slots()

        @pl.when(t == 2)
        def _():
            prepare_zeta()

        @pl.when(t == 0)
        def _():
            for side in range(2):
                for c in range(SIDE):
                    send_first(c, side).wait_recv()

        @pl.when(t > 0)
        def _():
            for side in range(2):
                send_halo(t, side).wait_recv()

        assemble(t)
        send_edge(t).start()

        @pl.when(t >= 2)
        def _():
            finish(t - 2)

        send_edge(t).wait_recv()
        sweep(t)

    @pl.loop(chunks - 2, chunks)
    def _(k):
        finish(k)

    both = jnp.concatenate(split(stokes[...]), axis=1)
    parts = 4
    per = tiles // parts
    for step in range(parts):
        part = lax.rem(place // per + step, parts)
        term = jnp.dot(
            placer[pl.ds(pl.multiple_of(part * per * slots, LANES), per * slots), :],
            both,
            preferred_element_type=f32,
        )
        posted[pl.ds(part * per, per)] = (term[:, :LANES] + term[:, LANES:]).reshape(
            per, slots, LANES
        )

        @pl.loop(1 if step == 0 else 0, per)
        def _(d):
            post(part * per + lax.rem(place + d, per)).start()

    arrived[place] = posted[place]

    @pl.loop(0, chunks)
    def _(k):
        for d in (1, 2, 3):
            send_in(k, d).wait_send()
            send_out(k, d).wait_send()
        send_edge(k).wait_send()
        store(k).wait()

    @pl.loop(1, chunks)
    def _(k):
        for side in range(2):
            send_halo(k, side).wait_send()

    for side in range(2):
        for c in range(SIDE):
            send_first(c, side).wait_send()

    def all_of(ref, sem):
        some = ref.at[pl.ds(0, tiles - 1)]
        return pltpu.make_async_copy(some, some, sem)

    all_of(arrived, post_recv).wait()
    arrived_out[...] = arrived[...].reshape(tiles * slots, LANES)
    all_of(posted, post_send).wait()


def split(value):
    high = value.astype(jnp.bfloat16)
    return high, (value - high.astype(jnp.float32)).astype(jnp.bfloat16)


def ocean_kernel(profiles, waves, zeta, coriolis, velocity, out_hbm, velocity_out, give_sem):
    f32 = jnp.float32
    pieces = give_sem.shape[0]
    span = waves.shape[0] // pieces

    def give(i):
        at = pl.ds(i * span, span)
        return pltpu.make_async_copy(waves.at[at], out_hbm.at[at], give_sem.at[i])

    for i in range(pieces):
        give(i).start()
    levels, cols = zeta.shape
    drifts = 2 * levels
    rows_in = profiles[...]
    target = rows_in[:, drifts : drifts + 1]
    column = lax.broadcasted_iota(jnp.int32, (rows_in.shape[0], cols), 1).astype(f32) + 1.0
    chosen = (target == column).astype(jnp.bfloat16)
    summed = lax.dot_general(
        jnp.concatenate(split(rows_in), axis=1),
        chosen,
        (((0,), (0,)), ((), ())),
        preferred_element_type=f32,
    )
    summed = summed[:LANES] + summed[LANES:]
    count = jnp.maximum(summed[drifts + 1 : drifts + 2], 1.0)
    east_drift = summed[:levels] / count
    north_drift = summed[levels:drifts] / count
    spin = coriolis[...]
    turn = spin + zeta[...]
    east, north = velocity[0], velocity[1]
    velocity_out[0] = east + 0.25 * (spin * north + turn * north_drift)
    velocity_out[1] = north - 0.25 * (spin * east + turn * east_drift)
    for i in range(pieces):
        give(i).wait()


def per_device(
    spectrum,
    interaction,
    comp_speed,
    sea_mask,
    stokes_kernel,
    tile_owner,
    ocean_column,
    neighbours,
    coriolis,
    velocity,
):
    held, comps = spectrum.shape[1:]
    chunks = comps // LANES
    rows = held // SIDE
    tall = rows + 2 * SIDE
    tiles = lax.axis_size("pts")
    slots = 16
    levels, cols = velocity.shape[2:]
    f32, bf16 = jnp.float32, jnp.bfloat16
    piece = pltpu.VMEM((chunks, SIDE, rows, LANES), f32)
    mask = pltpu.VMEM((tall * SUB, LANES), f32)
    vmem = pl.BlockSpec(memory_space=pltpu.VMEM)
    anywhere = pl.BlockSpec(memory_space=pl.ANY)
    hbm = pl.BlockSpec(memory_space=pltpu.HBM)
    dma = pltpu.SemaphoreType.DMA
    waves, profiles, zeta = pl.pallas_call(
        wave_kernel,
        out_shape=(
            jax.ShapeDtypeStruct((held, comps), f32),
            jax.ShapeDtypeStruct((tiles * slots, LANES), f32),
            jax.ShapeDtypeStruct((levels, cols), f32),
        ),
        in_specs=[hbm] * 9,
        out_specs=(anywhere, vmem, vmem),
        scratch_shapes=[
            pltpu.VMEM(sea_mask.shape, sea_mask.dtype),
            pltpu.VMEM(stokes_kernel.shape[::-1], f32),
            pltpu.VMEM((2, levels, cols), f32),
            pltpu.VMEM(comp_speed.shape, f32),
            pltpu.VMEM((1, held), jnp.int32),
            pltpu.VMEM((1, held), jnp.int32),
            pltpu.VMEM((neighbours.shape[2], cols), jnp.int32),
            pltpu.VMEM((chunks, held, LANES), f32),
            pltpu.VMEM((chunks, comps, LANES), bf16),
            pltpu.VMEM((held, comps), bf16),
            piece,
            piece,
            piece,
            piece,
            pltpu.VMEM((chunks, tall * SUB, LANES), f32),
            mask,
            piece,
            piece,
            pltpu.VMEM((chunks, held, LANES), f32),
            pltpu.VMEM((2, tall * SUB, LANES), f32),
            pltpu.VMEM((2, tall * SUB, LANES), f32),
            mask,
            pltpu.VMEM((2 * rows, GC), f32),
            pltpu.VMEM((chunks, 2 * LANES, 2 * LANES), bf16),
            pltpu.VMEM((held, LANES), f32),
            pltpu.VMEM((tiles * slots, held), bf16),
            pltpu.VMEM((tiles, slots, LANES), f32),
            pltpu.VMEM((tiles, slots, LANES), f32),
            dma((2, chunks)),
            dma((7,)),
            dma((chunks,)),
            dma((chunks, 3)),
            dma((chunks, 3)),
            dma((chunks, 2)),
            dma((chunks, 2)),
            dma((chunks,)),
            dma((chunks,)),
            dma((chunks, 3)),
            dma((chunks, 3)),
            dma(()),
            dma(()),
            dma((SIDE, 2)),
            dma((SIDE, 2)),
        ],
        compiler_params=pltpu.CompilerParams(
            collective_id=0, has_side_effects=True, vmem_limit_bytes=36 << 20
        ),
        name="wave_step",
    )(
        *(
            pltpu.with_memory_space_constraint(each, pltpu.HBM)
            for each in (
                spectrum[0],
                interaction,
                sea_mask,
                stokes_kernel.T,
                velocity[0],
                comp_speed,
                tile_owner.reshape(1, held),
                ocean_column,
                neighbours[0].T,
            )
        )
    )
    spectrum_next, velocity_next = pl.pallas_call(
        ocean_kernel,
        out_shape=(
            jax.ShapeDtypeStruct((held, comps), f32),
            jax.ShapeDtypeStruct((2, levels, cols), f32),
        ),
        in_specs=[vmem] * 5,
        out_specs=(hbm, vmem),
        scratch_shapes=[dma((SIDE,))],
        compiler_params=pltpu.CompilerParams(vmem_limit_bytes=8 << 20),
        name="ocean_step",
    )(profiles, waves, zeta, coriolis, velocity[0])
    return (spectrum_next[None], velocity_next[None])


def solution(mesh):
    placed = (
        P("grid", "pts", None),
        P(),
        P(),
        P(),
        P(),
        P("grid", "pts", None),
        P("grid", "pts"),
        P("grid", "pts", None),
        P("grid", "pts"),
        P("grid", None, None, "pts"),
    )
    return jax.shard_map(
        per_device,
        mesh=mesh,
        in_specs=placed,
        out_specs=(P("grid", "pts", None), P("grid", None, None, "pts")),
        check_vma=False,
    )
```

```python
import jax
import jax.numpy as jnp
from jax import lax
from jax.experimental import pallas as pl
from jax.experimental.pallas import tpu as pltpu
from jax.sharding import PartitionSpec as P

MESH = pl.DeviceIdType.MESH
LANES = 128
SUB = 8
SIDE = 4
GC = 256


def wave_kernel(
    spec_hbm,
    inter_hbm,
    sea_hbm,
    kern_hbm,
    velocity_hbm,
    speed_hbm,
    owner_hbm,
    ocean_hbm,
    near_hbm,
    out_hbm,
    arrived_out,
    zeta,
    sea,
    kern,
    velocity,
    speed,
    owner,
    ocean,
    near,
    spec,
    inter,
    half,
    sent,
    own,
    left,
    right,
    wide,
    swept,
    back,
    home,
    final,
    mask_pos,
    mask_neg,
    mask_now,
    sea_rows,
    drift_kernel,
    stokes,
    placer,
    posted,
    arrived,
    load_sem,
    side_sem,
    store_sem,
    in_send,
    in_recv,
    halo_send,
    halo_recv,
    edge_send,
    edge_recv,
    out_send,
    out_recv,
    post_send,
    post_recv,
    first_send,
    first_recv,
):
    f32, bf16, i32 = jnp.float32, jnp.bfloat16, jnp.int32
    chunks, held = spec.shape[:2]
    rows = held // SIDE
    tall = rows + 2 * SIDE
    tiles = arrived.shape[0]
    drifts = kern.shape[0]
    slots = arrived_out.shape[0] // tiles
    parts = 4
    per = tiles // parts
    cols = near.shape[1]
    grid = lax.axis_index("grid")
    place = lax.axis_index("pts")
    y = lax.rem(place, SIDE)
    base = place - y
    rings = tiles // SIDE
    ring = place // SIDE
    peers = [base + lax.rem(y + d, SIDE) for d in (1, 2, 3)]
    lanes = lambda k: pl.ds(pl.multiple_of(k * LANES, LANES), LANES)

    def turned(k, r):
        return (r - (k + k // 3) + rings - 1) // rings

    def group(k):
        return lax.rem(y - turned(k, ring) + SIDE, SIDE)

    def block(k):
        return rings * group(k) + ring

    def beside(k, step):
        other = lax.rem(ring + step + rings, rings)
        across = (ring + step + rings) // rings - 1
        turn = across + turned(k, other) - turned(k, ring)
        return SIDE * other + lax.rem(y + turn + 2 * SIDE, SIDE)

    def load_spec(k):
        return pltpu.make_async_copy(spec_hbm.at[:, lanes(k)], spec.at[k], load_sem.at[0, k])

    def load_inter(k):
        return pltpu.make_async_copy(inter_hbm.at[:, lanes(k)], inter.at[k], load_sem.at[1, k])

    barrier = pltpu.get_barrier_semaphore()

    @pl.loop(1, tiles)
    def _(d):
        pl.semaphore_signal(
            barrier, inc=1, device_id={"pts": lax.rem(place + d, tiles)}, device_id_type=MESH
        )

    pl.semaphore_signal(barrier, inc=1, device_id={"grid": 1 - grid}, device_id_type=MESH)

    @pl.loop(0, chunks)
    def _(k):
        load_spec(k).start()

    @pl.loop(0, chunks)
    def _(k):
        load_inter(k).start()

    side_loads = [
        pltpu.make_async_copy(source, target, side_sem.at[i])
        for i, (source, target) in enumerate(
            [
                (sea_hbm, sea),
                (kern_hbm, kern),
                (velocity_hbm, velocity),
                (speed_hbm, speed),
                (owner_hbm, owner),
                (ocean_hbm, ocean),
                (near_hbm, near),
            ]
        )
    ]
    for each in side_loads:
        each.start()

    for k in range(chunks):
        load_spec(k).wait()
        for m in range(SIDE):
            half[m * rows : (m + 1) * rows, k * LANES : (k + 1) * LANES] = spec[
                k, pl.ds(m, rows, stride=SIDE), :
            ].astype(bf16)

    def send_in(k, d):
        return pltpu.make_async_remote_copy(
            src_ref=sent.at[k, lax.rem(group(k) + d, SIDE)],
            dst_ref=own.at[k, y],
            send_sem=in_send.at[k, d - 1],
            recv_sem=in_recv.at[k, d - 1],
            device_id={"pts": peers[d - 1]},
            device_id_type=MESH,
        )

    def send_halo(k, side):
        return pltpu.make_async_remote_copy(
            src_ref=own.at[k],
            dst_ref=(left if side == 0 else right).at[k],
            send_sem=halo_send.at[k, side],
            recv_sem=halo_recv.at[k, side],
            device_id={"pts": beside(k, 1 if side == 0 else -1)},
            device_id_type=MESH,
        )

    early = first_send.shape[0]

    def send_first(k, c, side):
        return pltpu.make_async_remote_copy(
            src_ref=own.at[k, c],
            dst_ref=(left if side == 0 else right).at[k, c],
            send_sem=first_send.at[k, c, side],
            recv_sem=first_recv.at[k, c, side],
            device_id={"pts": beside(k, 1 if side == 0 else -1)},
            device_id_type=MESH,
        )

    def send_edge(k):
        at = pl.multiple_of((rows - (rows - SIDE) * grid) * SUB, SUB)
        to = pl.multiple_of((rows + SIDE) * SUB * grid, SUB)
        return pltpu.make_async_remote_copy(
            src_ref=wide.at[k, pl.ds(at, SIDE * SUB)],
            dst_ref=wide.at[k, pl.ds(to, SIDE * SUB)],
            send_sem=edge_send.at[k],
            recv_sem=edge_recv.at[k],
            device_id={"grid": 1 - grid},
            device_id_type=MESH,
        )

    def send_out(k, d):
        return pltpu.make_async_remote_copy(
            src_ref=back.at[k, lax.rem(y + d, SIDE)],
            dst_ref=home.at[k, group(k)],
            send_sem=out_send.at[k, d - 1],
            recv_sem=out_recv.at[k, d - 1],
            device_id={"pts": peers[d - 1]},
            device_id_type=MESH,
        )

    def post(peer):
        return pltpu.make_async_remote_copy(
            src_ref=posted.at[peer],
            dst_ref=arrived.at[place],
            send_sem=post_send,
            recv_sem=post_recv,
            device_id={"pts": peer},
            device_id_type=MESH,
        )

    def store(k):
        return pltpu.make_async_copy(final.at[k], out_hbm.at[:, lanes(k)], store_sem.at[k])

    def relax(k):
        load_inter(k).wait()
        mix = jnp.dot(half[...], inter[k], preferred_element_type=f32)
        grown = jnp.tanh(mix)
        for m in range(SIDE):
            local = spec[k, pl.ds(m, rows, stride=SIDE), :]
            sent[k, m] = local + 0.5 * local * grown[m * rows : (m + 1) * rows]
        own[k, y] = sent[k, group(k)]

    def launch(k):
        for d in (2, 1, 3):
            send_in(k, d).start()

    def forward(k):
        for d in (1, 2, 3):
            send_in(k, d).wait_recv()
        for side in range(2):
            send_halo(k, side).start()

    def prepare_masks():
        @pl.loop(0, rows)
        def _(r):
            pair = sea[:, pl.ds(pl.multiple_of(r * GC, GC), GC)].astype(f32)
            sea_rows[pl.ds(r, 1), :] = pair[0:1]
            sea_rows[pl.ds(r + rows, 1), :] = pair[1:2]

        row_at = lax.broadcasted_iota(i32, (tall, 2 * rows), 0) + (rows * grid - SIDE)
        row_of = lax.broadcasted_iota(i32, (tall, 2 * rows), 1)
        picked = jnp.dot(
            (row_at == row_of).astype(bf16),
            sea_rows[...].astype(bf16),
            preferred_element_type=f32,
        ).astype(bf16)
        column = lax.broadcasted_iota(i32, (GC, LANES), 0)
        for turn in range(2):
            start = SIDE * (rings * lax.rem(y - turn + SIDE, SIDE) + ring)
            for s in range(SUB):
                first = (column == start - SIDE + s).astype(bf16)
                second = (column == start + 7 - s).astype(bf16)
                mask_pos[turn, pl.ds(s, tall, stride=SUB), :] = jnp.dot(
                    picked, first, preferred_element_type=f32
                )
                mask_neg[turn, pl.ds(s, tall, stride=SUB), :] = jnp.dot(
                    picked, second, preferred_element_type=f32
                )

    def prepare_kernel():
        drift_kernel[...] = jnp.zeros_like(drift_kernel)
        for k in range(chunks):
            high, low = split(kern[:, k * LANES : (k + 1) * LANES])
            drift_kernel[k, 0:drifts, 0:LANES] = high
            drift_kernel[k, 0:drifts, LANES : 2 * LANES] = high
            drift_kernel[k, LANES : LANES + drifts, 0:LANES] = low

    def prepare_slots():
        down = lax.broadcasted_iota(i32, (held, held), 0)
        across = lax.broadcasted_iota(i32, (held, held), 1)
        owner_row = owner[...].astype(f32)
        owners = jnp.broadcast_to(owner_row, (held, held))
        owner_column = jnp.sum(jnp.where(down == across, owners, 0.0), axis=1, keepdims=True)
        earlier = (owners == owner_column) & (down < across)
        rank = jnp.sum(jnp.where(earlier, 1.0, 0.0), axis=0, keepdims=True)
        quarter = jnp.floor(owner_row / per)
        slot = (quarter * slots + rank) * per + (owner_row - quarter * per)
        for part in range(tiles * slots // LANES):
            at = lax.broadcasted_iota(i32, (LANES, held), 0) + part * LANES
            placer[part * LANES : (part + 1) * LANES, :] = (at.astype(f32) == slot).astype(bf16)
        wanted = jnp.broadcast_to(ocean[...].astype(f32) + 1.0, (held, held))
        target = jnp.sum(jnp.where(down == across, wanted, 0.0), axis=1, keepdims=True)
        lane = lax.broadcasted_iota(i32, (held, LANES), 1)
        stokes[...] = jnp.where(lane == drifts, target, 0.0)

    def prepare_zeta():
        column = lax.broadcasted_iota(i32, (cols, cols), 0)

        def apart(first, second):
            one = (near[first : first + 1, :] == column).astype(f32)
            two = (near[second : second + 1, :] == column).astype(f32)
            return (one - two).astype(bf16)

        def taken(flow, picker):
            high, low = split(flow)
            rest = (flow - high.astype(f32) - low.astype(f32)).astype(bf16)
            total = jnp.zeros(flow.shape, f32)
            for each in (high, low, rest):
                total += jnp.dot(each, picker, preferred_element_type=f32)
            return total

        zeta[...] = taken(velocity[1], apart(0, 1)) - taken(velocity[0], apart(2, 3))

    def assemble(k):
        pos = jnp.broadcast_to(speed[1:2, lanes(k)] > 0.0, (rows, LANES))
        from_left = block(k) > 0
        from_right = block(k) < tiles - 1
        for s in range(SIDE):
            lower = jnp.where(from_left, left[k, s], 0.0)
            upper = jnp.where(from_right, right[k, SIDE - 1 - s], 0.0)
            wide[k, pl.ds(SIDE * SUB + s, rows, stride=SUB), :] = jnp.where(pos, lower, upper)
        for q in range(SIDE):
            wide[k, pl.ds(SIDE * SUB + SIDE + q, rows, stride=SUB), :] = jnp.where(
                pos, own[k, q], own[k, SIDE - 1 - q]
            )
        outside = pl.multiple_of((rows + SIDE) * SUB * grid, SUB)
        wide[k, pl.ds(outside, SIDE * SUB), :] = jnp.zeros((SIDE * SUB, LANES), f32)

    def sweep(k):
        spread = lambda v: jnp.broadcast_to(v, (SUB, LANES))
        cx = speed[0:1, lanes(k)]
        cy = speed[1:2, lanes(k)]
        down_rate = spread(jnp.maximum(cx, 0.0))
        up_rate = spread(jnp.maximum(-cx, 0.0))
        side_rate = spread(jnp.abs(cy))
        keep = 1.0 - down_rate - up_rate - side_rate
        pos = spread(cy) > 0.0
        turn = turned(k, ring)

        @pl.loop(0, tall // SUB)
        def _(part):
            for u in range(SUB):
                at = pl.ds(pl.multiple_of((part * SUB + u) * SUB, SUB), SUB)
                mask_now[at, :] = jnp.where(pos, mask_pos[turn, at, :], mask_neg[turn, at, :])

        zero = jnp.zeros((SUB, LANES), f32)

        def part(i, carry):
            held_rows = [list(pair) for pair in carry[0]]
            masks = list(carry[1])
            for u in range(SUB):
                at = pl.ds(pl.multiple_of((i * SUB + u) * SUB, SUB), SUB)
                value = wide[k, at, :]
                for stage in range(SIDE):
                    previous, current = held_rows[stage]
                    moved = (
                        keep * current
                        + down_rate * previous
                        + up_rate * value
                        + side_rate * pltpu.roll(current, 1, 0)
                    )
                    held_rows[stage] = [current, value]
                    value = moved * masks[stage]
                swept[at, :] = value
                masks = [mask_now[at, :]] + masks[: SIDE - 1]
            return tuple(tuple(pair) for pair in held_rows), tuple(masks)

        start = (tuple((zero, zero) for _ in range(SIDE)), (zero,) * SIDE)
        lax.fori_loop(0, tall // SUB, part, start)
        wanted = jnp.broadcast_to(cy > 0.0, (rows, LANES))
        columns = [
            swept[pl.ds(2 * SIDE * SUB + SIDE + q, rows, stride=SUB), :] for q in range(SIDE)
        ]
        for c in range(SIDE):
            back[k, c] = jnp.where(wanted, columns[c], columns[SIDE - 1 - c])
        home[k, group(k)] = back[k, y]
        for d in (2, 1, 3):
            send_out(k, d).start()

    def finish(k):
        for d in (1, 2, 3):
            send_out(k, d).wait_recv()
        for m in range(SIDE):
            final[k, pl.ds(m, rows, stride=SIDE), :] = home[k, m]
        store(k).start()
        both = jnp.concatenate(split(final[k]), axis=1)
        term = lax.dot_general(
            both, drift_kernel[k], (((1,), (1,)), ((), ())), preferred_element_type=f32
        )
        stokes[...] += term[:, :LANES] + term[:, LANES:]

    relax(0)
    pl.semaphore_wait(barrier, tiles)
    for k in range(early):
        if k > 0:
            relax(k)
        launch(k)
        for side in range(2):
            send_first(k, y, side).start()
    ahead = 6
    for k in range(early, ahead - early + 1):
        relax(k)
        launch(k)
    for k in range(early):
        for d in (1, 3, 2):
            send_in(k, d).wait_recv()
            for side in range(2):
                send_first(k, lax.rem(y - d + SIDE, SIDE), side).start()
        if ahead - early + 1 + k < ahead:
            relax(ahead - early + 1 + k)
            launch(ahead - early + 1 + k)

    for each in side_loads:
        each.wait()
    prepare_masks()

    @pl.loop(0, chunks)
    def _(t):
        @pl.when(t + 3 + 3 < chunks)
        def _():
            relax(t + 3 + 3)
            launch(t + 3 + 3)

        @pl.when(t + 3 < chunks)
        def _():
            forward(t + 3)

        @pl.when(t == 0)
        def _():
            prepare_kernel()

        @pl.when(t == 1)
        def _():
            prepare_slots()

        @pl.when(t == 2)
        def _():
            prepare_zeta()

        @pl.when(t < early)
        def _():
            for side in range(2):
                for c in range(SIDE):
                    send_first(t, c, side).wait_recv()

        @pl.when(t >= early)
        def _():
            for side in range(2):
                send_halo(t, side).wait_recv()

        assemble(t)
        send_edge(t).start()

        @pl.when(t >= 2)
        def _():
            finish(t - 2)

        send_edge(t).wait_recv()
        sweep(t)

    @pl.loop(chunks - 2, chunks)
    def _(k):
        finish(k)

    starts = [divmod(i * (drifts + 1), LANES) for i in range(slots)]
    both = jnp.concatenate(split(stokes[...]), axis=1)
    lane = lax.broadcasted_iota(jnp.int32, (per, LANES), 1)
    for step in range(parts):
        part = lax.rem(place // per + step, parts)
        term = jnp.dot(
            placer[pl.ds(pl.multiple_of(part * per * slots, 2 * SUB), per * slots), :],
            both,
            preferred_element_type=f32,
        )
        packed = [jnp.zeros((per, LANES), f32) for _ in range(arrived.shape[1])]
        for i, (row, at) in enumerate(starts):
            mine = term[i * per : (i + 1) * per]
            mine = mine[:, :LANES] + mine[:, LANES:]
            if at:
                mine = pltpu.roll(mine, at, 1)
            end = at + drifts + 1
            packed[row] = jnp.where((lane >= at) & (lane < end), mine, packed[row])
            if end > LANES:
                packed[row + 1] = jnp.where(lane < end - LANES, mine, packed[row + 1])
        for row, values in enumerate(packed):
            posted[pl.ds(part * per, per), row, :] = values

        @pl.loop(1 if step == 0 else 0, per)
        def _(d):
            post(part * per + lax.rem(place + d, per)).start()

    arrived[place] = posted[place]

    @pl.loop(0, chunks)
    def _(k):
        for d in (1, 2, 3):
            send_in(k, d).wait_send()
            send_out(k, d).wait_send()
        send_edge(k).wait_send()
        store(k).wait()

    @pl.loop(early, chunks)
    def _(k):
        for side in range(2):
            send_halo(k, side).wait_send()

    @pl.loop(0, early)
    def _(k):
        for side in range(2):
            for c in range(SIDE):
                send_first(k, c, side).wait_send()

    def all_of(ref, sem):
        some = ref.at[pl.ds(0, tiles - 1)]
        return pltpu.make_async_copy(some, some, sem)

    all_of(arrived, post_recv).wait()
    lane = lax.broadcasted_iota(jnp.int32, (tiles, LANES), 1)
    for i, (row, at) in enumerate(starts):
        taken = arrived[:, row, :]
        if at + drifts + 1 > LANES:
            taken = jnp.where(lane >= at, taken, arrived[:, row + 1, :])
        if at:
            taken = pltpu.roll(taken, LANES - at, 1)
        arrived_out[i * tiles : (i + 1) * tiles, :] = jnp.where(lane == drifts + 1, 1.0, taken)
    all_of(posted, post_send).wait()


def split(value):
    high = value.astype(jnp.bfloat16)
    return high, (value - high.astype(jnp.float32)).astype(jnp.bfloat16)


def ocean_kernel(profiles, waves, zeta, coriolis, velocity, out_hbm, velocity_out, give_sem):
    f32 = jnp.float32
    pieces = give_sem.shape[0]
    span = waves.shape[0] // pieces

    def give(i):
        at = pl.ds(i * span, span)
        return pltpu.make_async_copy(waves.at[at], out_hbm.at[at], give_sem.at[i])

    for i in range(pieces):
        give(i).start()
    levels, cols = zeta.shape
    drifts = 2 * levels
    rows_in = profiles[...]
    target = rows_in[:, drifts : drifts + 1]
    column = lax.broadcasted_iota(jnp.int32, (rows_in.shape[0], cols), 1).astype(f32) + 1.0
    chosen = (target == column).astype(jnp.bfloat16)
    summed = lax.dot_general(
        jnp.concatenate(split(rows_in), axis=1),
        chosen,
        (((0,), (0,)), ((), ())),
        preferred_element_type=f32,
    )
    summed = summed[:LANES] + summed[LANES:]
    count = jnp.maximum(summed[drifts + 1 : drifts + 2], 1.0)
    east_drift = summed[:levels] / count
    north_drift = summed[levels:drifts] / count
    spin = coriolis[...]
    turn = spin + zeta[...]
    east, north = velocity[0], velocity[1]
    velocity_out[0] = east + 0.25 * (spin * north + turn * north_drift)
    velocity_out[1] = north - 0.25 * (spin * east + turn * east_drift)
    for i in range(pieces):
        give(i).wait()


def per_device(
    spectrum,
    interaction,
    comp_speed,
    sea_mask,
    stokes_kernel,
    tile_owner,
    ocean_column,
    neighbours,
    coriolis,
    velocity,
):
    held, comps = spectrum.shape[1:]
    chunks = comps // LANES
    rows = held // SIDE
    tall = rows + 2 * SIDE
    tiles = lax.axis_size("pts")
    slots = 2 * held // tiles
    levels, cols = velocity.shape[2:]
    packed = -(-slots * (2 * levels + 1) // LANES)
    f32, bf16 = jnp.float32, jnp.bfloat16
    piece = pltpu.VMEM((chunks, SIDE, rows, LANES), f32)
    mask = pltpu.VMEM((tall * SUB, LANES), f32)
    vmem = pl.BlockSpec(memory_space=pltpu.VMEM)
    anywhere = pl.BlockSpec(memory_space=pl.ANY)
    hbm = pl.BlockSpec(memory_space=pltpu.HBM)
    dma = pltpu.SemaphoreType.DMA
    waves, profiles, zeta = pl.pallas_call(
        wave_kernel,
        out_shape=(
            jax.ShapeDtypeStruct((held, comps), f32),
            jax.ShapeDtypeStruct((tiles * slots, LANES), f32),
            jax.ShapeDtypeStruct((levels, cols), f32),
        ),
        in_specs=[hbm] * 9,
        out_specs=(anywhere, vmem, vmem),
        scratch_shapes=[
            pltpu.VMEM(sea_mask.shape, sea_mask.dtype),
            pltpu.VMEM(stokes_kernel.shape[::-1], f32),
            pltpu.VMEM((2, levels, cols), f32),
            pltpu.VMEM(comp_speed.shape, f32),
            pltpu.VMEM((1, held), jnp.int32),
            pltpu.VMEM((1, held), jnp.int32),
            pltpu.VMEM((neighbours.shape[2], cols), jnp.int32),
            pltpu.VMEM((chunks, held, LANES), f32),
            pltpu.VMEM((chunks, comps, LANES), bf16),
            pltpu.VMEM((held, comps), bf16),
            piece,
            piece,
            piece,
            piece,
            pltpu.VMEM((chunks, tall * SUB, LANES), f32),
            mask,
            piece,
            piece,
            pltpu.VMEM((chunks, held, LANES), f32),
            pltpu.VMEM((2, tall * SUB, LANES), f32),
            pltpu.VMEM((2, tall * SUB, LANES), f32),
            mask,
            pltpu.VMEM((2 * rows, GC), f32),
            pltpu.VMEM((chunks, 2 * LANES, 2 * LANES), bf16),
            pltpu.VMEM((held, LANES), f32),
            pltpu.VMEM((tiles * slots, held), bf16),
            pltpu.VMEM((tiles, packed, LANES), f32),
            pltpu.VMEM((tiles, packed, LANES), f32),
            dma((2, chunks)),
            dma((7,)),
            dma((chunks,)),
            dma((chunks, 3)),
            dma((chunks, 3)),
            dma((chunks, 2)),
            dma((chunks, 2)),
            dma((chunks,)),
            dma((chunks,)),
            dma((chunks, 3)),
            dma((chunks, 3)),
            dma(()),
            dma(()),
            dma((3, SIDE, 2)),
            dma((3, SIDE, 2)),
        ],
        compiler_params=pltpu.CompilerParams(
            collective_id=0, has_side_effects=True, vmem_limit_bytes=36 << 20
        ),
        name="wave_step",
    )(
        *(
            pltpu.with_memory_space_constraint(each, pltpu.HBM)
            for each in (
                spectrum[0],
                interaction,
                sea_mask,
                stokes_kernel.T,
                velocity[0],
                comp_speed,
                tile_owner.reshape(1, held),
                ocean_column,
                neighbours[0].T,
            )
        )
    )
    spectrum_next, velocity_next = pl.pallas_call(
        ocean_kernel,
        out_shape=(
            jax.ShapeDtypeStruct((held, comps), f32),
            jax.ShapeDtypeStruct((2, levels, cols), f32),
        ),
        in_specs=[vmem] * 5,
        out_specs=(hbm, vmem),
        scratch_shapes=[dma((SIDE,))],
        compiler_params=pltpu.CompilerParams(vmem_limit_bytes=8 << 20),
        name="ocean_step",
    )(profiles, waves, zeta, coriolis, velocity[0])
    return (spectrum_next[None], velocity_next[None])


def solution(mesh):
    placed = (
        P("grid", "pts", None),
        P(),
        P(),
        P(),
        P(),
        P("grid", "pts", None),
        P("grid", "pts"),
        P("grid", "pts", None),
        P("grid", "pts"),
        P("grid", None, None, "pts"),
    )
    return jax.shard_map(
        per_device,
        mesh=mesh,
        in_specs=placed,
        out_specs=(P("grid", "pts", None), P("grid", None, None, "pts")),
        check_vma=False,
    )
```

```python
import jax
import jax.numpy as jnp
from jax import lax
from jax.experimental import pallas as pl
from jax.experimental.pallas import tpu as pltpu
from jax.sharding import PartitionSpec as P

MESH = pl.DeviceIdType.MESH
LANES = 128
SUB = 8
SIDE = 4
GC = 256


def wave_kernel(
    spec_hbm,
    inter_hbm,
    sea_hbm,
    kern_hbm,
    velocity_hbm,
    speed_hbm,
    owner_hbm,
    ocean_hbm,
    near_hbm,
    out_hbm,
    arrived_out,
    zeta,
    sea,
    kern,
    velocity,
    speed,
    owner,
    ocean,
    near,
    spec,
    inter,
    half,
    sent,
    own,
    left,
    right,
    wide,
    swept,
    back,
    home,
    final,
    mask_pos,
    mask_neg,
    mask_now,
    sea_rows,
    drift_kernel,
    stokes,
    placer,
    posted,
    arrived,
    load_sem,
    side_sem,
    store_sem,
    in_send,
    in_recv,
    halo_send,
    halo_recv,
    edge_send,
    edge_recv,
    out_send,
    out_recv,
    post_send,
    post_recv,
    first_send,
    first_recv,
):
    f32, bf16, i32 = jnp.float32, jnp.bfloat16, jnp.int32
    chunks, held = spec.shape[:2]
    rows = held // SIDE
    tall = rows + 2 * SIDE
    tiles = arrived.shape[0]
    drifts = kern.shape[0]
    slots = arrived_out.shape[0] // tiles
    parts = 4
    per = tiles // parts
    cols = near.shape[1]
    grid = lax.axis_index("grid")
    place = lax.axis_index("pts")
    y = lax.rem(place, SIDE)
    base = place - y
    rings = tiles // SIDE
    ring = place // SIDE
    peers = [base + lax.rem(y + d, SIDE) for d in (1, 2, 3)]
    lanes = lambda k: pl.ds(pl.multiple_of(k * LANES, LANES), LANES)

    def turned(k, r):
        return (r - (k + k // 3) + rings - 1) // rings

    def group(k):
        return lax.rem(y - turned(k, ring) + SIDE, SIDE)

    def block(k):
        return rings * group(k) + ring

    def beside(k, step):
        other = lax.rem(ring + step + rings, rings)
        across = (ring + step + rings) // rings - 1
        turn = across + turned(k, other) - turned(k, ring)
        return SIDE * other + lax.rem(y + turn + 2 * SIDE, SIDE)

    def load_spec(k):
        return pltpu.make_async_copy(spec_hbm.at[:, lanes(k)], spec.at[k], load_sem.at[0, k])

    def load_inter(k):
        return pltpu.make_async_copy(inter_hbm.at[:, lanes(k)], inter.at[k], load_sem.at[1, k])

    @pl.loop(0, chunks)
    def _(k):
        load_spec(k).start()

    load_inter(0).start()
    barrier = pltpu.get_barrier_semaphore()

    @pl.loop(1, tiles)
    def _(d):
        pl.semaphore_signal(
            barrier, inc=1, device_id={"pts": lax.rem(place + d, tiles)}, device_id_type=MESH
        )

    pl.semaphore_signal(barrier, inc=1, device_id={"grid": 1 - grid}, device_id_type=MESH)

    @pl.loop(1, chunks)
    def _(k):
        load_inter(k).start()

    side_loads = [
        pltpu.make_async_copy(source, target, side_sem.at[i])
        for i, (source, target) in enumerate(
            [
                (sea_hbm, sea),
                (kern_hbm, kern),
                (velocity_hbm, velocity),
                (speed_hbm, speed),
                (owner_hbm, owner),
                (ocean_hbm, ocean),
                (near_hbm, near),
            ]
        )
    ]
    for each in side_loads:
        each.start()

    for k in range(chunks):
        load_spec(k).wait()
        for m in range(SIDE):
            half[m * rows : (m + 1) * rows, k * LANES : (k + 1) * LANES] = spec[
                k, pl.ds(m, rows, stride=SIDE), :
            ].astype(bf16)

    def send_in(k, d):
        return pltpu.make_async_remote_copy(
            src_ref=sent.at[k, lax.rem(group(k) + d, SIDE)],
            dst_ref=own.at[k, y],
            send_sem=in_send.at[k, d - 1],
            recv_sem=in_recv.at[k, d - 1],
            device_id={"pts": peers[d - 1]},
            device_id_type=MESH,
        )

    def send_halo(k, side):
        return pltpu.make_async_remote_copy(
            src_ref=own.at[k],
            dst_ref=(left if side == 0 else right).at[k],
            send_sem=halo_send.at[k, side],
            recv_sem=halo_recv.at[k, side],
            device_id={"pts": beside(k, 1 if side == 0 else -1)},
            device_id_type=MESH,
        )

    early = first_send.shape[0]

    def send_first(k, c, side):
        return pltpu.make_async_remote_copy(
            src_ref=own.at[k, c],
            dst_ref=(left if side == 0 else right).at[k, c],
            send_sem=first_send.at[k, c, side],
            recv_sem=first_recv.at[k, c, side],
            device_id={"pts": beside(k, 1 if side == 0 else -1)},
            device_id_type=MESH,
        )

    def send_edge(k):
        at = pl.multiple_of((rows - (rows - SIDE) * grid) * SUB, SUB)
        to = pl.multiple_of((rows + SIDE) * SUB * grid, SUB)
        return pltpu.make_async_remote_copy(
            src_ref=wide.at[k, pl.ds(at, SIDE * SUB)],
            dst_ref=wide.at[k, pl.ds(to, SIDE * SUB)],
            send_sem=edge_send.at[k],
            recv_sem=edge_recv.at[k],
            device_id={"grid": 1 - grid},
            device_id_type=MESH,
        )

    def send_out(k, d):
        return pltpu.make_async_remote_copy(
            src_ref=back.at[k, lax.rem(y + d, SIDE)],
            dst_ref=home.at[k, group(k)],
            send_sem=out_send.at[k, d - 1],
            recv_sem=out_recv.at[k, d - 1],
            device_id={"pts": peers[d - 1]},
            device_id_type=MESH,
        )

    def post(peer):
        return pltpu.make_async_remote_copy(
            src_ref=posted.at[peer],
            dst_ref=arrived.at[place],
            send_sem=post_send,
            recv_sem=post_recv,
            device_id={"pts": peer},
            device_id_type=MESH,
        )

    def store(k):
        return pltpu.make_async_copy(final.at[k], out_hbm.at[:, lanes(k)], store_sem.at[k])

    def relax(k):
        load_inter(k).wait()
        mix = jnp.dot(half[...], inter[k], preferred_element_type=f32)
        grown = jnp.tanh(mix)
        for m in range(SIDE):
            local = spec[k, pl.ds(m, rows, stride=SIDE), :]
            sent[k, m] = local + 0.5 * local * grown[m * rows : (m + 1) * rows]
        own[k, y] = sent[k, group(k)]

    def launch(k):
        for d in (2, 1, 3):
            send_in(k, d).start()

    def forward(k):
        for d in (1, 2, 3):
            send_in(k, d).wait_recv()
        for side in range(2):
            send_halo(k, side).start()

    def prepare_masks():
        @pl.loop(0, rows)
        def _(r):
            pair = sea[:, pl.ds(pl.multiple_of(r * GC, GC), GC)].astype(f32)
            sea_rows[pl.ds(r, 1), :] = pair[0:1]
            sea_rows[pl.ds(r + rows, 1), :] = pair[1:2]

        row_at = lax.broadcasted_iota(i32, (tall, 2 * rows), 0) + (rows * grid - SIDE)
        row_of = lax.broadcasted_iota(i32, (tall, 2 * rows), 1)
        picked = jnp.dot(
            (row_at == row_of).astype(bf16),
            sea_rows[...].astype(bf16),
            preferred_element_type=f32,
        ).astype(bf16)
        column = lax.broadcasted_iota(i32, (GC, LANES), 0)
        for turn in range(2):
            start = SIDE * (rings * lax.rem(y - turn + SIDE, SIDE) + ring)
            for s in range(SUB):
                first = (column == start - SIDE + s).astype(bf16)
                second = (column == start + 7 - s).astype(bf16)
                mask_pos[turn, pl.ds(s, tall, stride=SUB), :] = jnp.dot(
                    picked, first, preferred_element_type=f32
                )
                mask_neg[turn, pl.ds(s, tall, stride=SUB), :] = jnp.dot(
                    picked, second, preferred_element_type=f32
                )

    def prepare_kernel():
        drift_kernel[...] = jnp.zeros_like(drift_kernel)
        for k in range(chunks):
            high, low = split(kern[:, k * LANES : (k + 1) * LANES])
            drift_kernel[k, 0:drifts, 0:LANES] = high
            drift_kernel[k, 0:drifts, LANES : 2 * LANES] = high
            drift_kernel[k, LANES : LANES + drifts, 0:LANES] = low

    def prepare_slots():
        down = lax.broadcasted_iota(i32, (held, held), 0)
        across = lax.broadcasted_iota(i32, (held, held), 1)
        owner_row = owner[...].astype(f32)
        owners = jnp.broadcast_to(owner_row, (held, held))
        owner_column = jnp.sum(jnp.where(down == across, owners, 0.0), axis=1, keepdims=True)
        earlier = (owners == owner_column) & (down < across)
        rank = jnp.sum(jnp.where(earlier, 1.0, 0.0), axis=0, keepdims=True)
        quarter = jnp.floor(owner_row / per)
        slot = (quarter * slots + rank) * per + (owner_row - quarter * per)
        for part in range(tiles * slots // LANES):
            at = lax.broadcasted_iota(i32, (LANES, held), 0) + part * LANES
            placer[part * LANES : (part + 1) * LANES, :] = (at.astype(f32) == slot).astype(bf16)
        wanted = jnp.broadcast_to(ocean[...].astype(f32) + 1.0, (held, held))
        target = jnp.sum(jnp.where(down == across, wanted, 0.0), axis=1, keepdims=True)
        lane = lax.broadcasted_iota(i32, (held, LANES), 1)
        stokes[...] = jnp.where(lane == drifts, target, 0.0)

    def prepare_zeta():
        column = lax.broadcasted_iota(i32, (cols, cols), 0)

        def apart(first, second):
            one = (near[first : first + 1, :] == column).astype(f32)
            two = (near[second : second + 1, :] == column).astype(f32)
            return (one - two).astype(bf16)

        def taken(flow, picker):
            high, low = split(flow)
            rest = (flow - high.astype(f32) - low.astype(f32)).astype(bf16)
            total = jnp.zeros(flow.shape, f32)
            for each in (high, low, rest):
                total += jnp.dot(each, picker, preferred_element_type=f32)
            return total

        zeta[...] = taken(velocity[1], apart(0, 1)) - taken(velocity[0], apart(2, 3))

    def set_out(k):
        pos = jnp.broadcast_to(speed[1:2, lanes(k)] > 0.0, (rows, LANES))
        for q in range(SIDE):
            wide[k, pl.ds(SIDE * SUB + SIDE + q, rows, stride=SUB), :] = jnp.where(
                pos, own[k, q], own[k, SIDE - 1 - q]
            )
        outside = pl.multiple_of((rows + SIDE) * SUB * grid, SUB)
        wide[k, pl.ds(outside, SIDE * SUB), :] = jnp.zeros((SIDE * SUB, LANES), f32)
        turn = turned(k, ring)
        each = jnp.broadcast_to(speed[1:2, lanes(k)], (SUB, LANES)) > 0.0

        @pl.loop(0, tall // SUB)
        def _(part):
            for u in range(SUB):
                at = pl.ds(pl.multiple_of((part * SUB + u) * SUB, SUB), SUB)
                mask_now[at, :] = jnp.where(each, mask_pos[turn, at, :], mask_neg[turn, at, :])

    def assemble(k):
        pos = jnp.broadcast_to(speed[1:2, lanes(k)] > 0.0, (rows, LANES))
        from_left = block(k) > 0
        from_right = block(k) < tiles - 1
        for s in range(SIDE):
            lower = jnp.where(from_left, left[k, s], 0.0)
            upper = jnp.where(from_right, right[k, SIDE - 1 - s], 0.0)
            wide[k, pl.ds(SIDE * SUB + s, rows, stride=SUB), :] = jnp.where(pos, lower, upper)

    def sweep(k):
        spread = lambda v: jnp.broadcast_to(v, (SUB, LANES))
        cx = speed[0:1, lanes(k)]
        cy = speed[1:2, lanes(k)]
        along = jnp.where(grid == 0, cx, -cx)
        behind_rate = spread(jnp.maximum(along, 0.0))
        front_rate = spread(jnp.maximum(-along, 0.0))
        side_rate = spread(jnp.abs(cy))
        keep = 1.0 - behind_rate - front_rate - side_rate
        zero = jnp.zeros((SUB, LANES), f32)

        def part(i, carry):
            held_rows = [list(pair) for pair in carry[0]]
            masks = list(carry[1])
            for u in range(SUB):
                r = i * SUB + u
                row = r + grid * (tall - 1 - 2 * r)
                at = pl.ds(pl.multiple_of(row * SUB, SUB), SUB)
                to = pl.ds(pl.multiple_of((row + grid * SUB) * SUB, SUB), SUB)
                value = wide[k, at, :]
                for stage in range(SIDE):
                    previous, current = held_rows[stage]
                    moved = (
                        keep * current
                        + behind_rate * previous
                        + front_rate * value
                        + side_rate * pltpu.roll(current, 1, 0)
                    )
                    held_rows[stage] = [current, value]
                    value = moved * masks[stage]
                swept[to, :] = value
                masks = [mask_now[at, :]] + masks[: SIDE - 1]
            return tuple(tuple(pair) for pair in held_rows), tuple(masks)

        start = (tuple((zero, zero) for _ in range(SIDE)), (zero,) * SIDE)
        nearly = lax.fori_loop(0, tall // SUB - 1, part, start)
        send_edge(k).wait_recv()
        part(tall // SUB - 1, nearly)
        wanted = jnp.broadcast_to(cy > 0.0, (rows, LANES))
        columns = [
            swept[pl.ds(2 * SIDE * SUB + SIDE + q, rows, stride=SUB), :] for q in range(SIDE)
        ]
        for c in range(SIDE):
            back[k, c] = jnp.where(wanted, columns[c], columns[SIDE - 1 - c])
        home[k, group(k)] = back[k, y]
        for d in (2, 1, 3):
            send_out(k, d).start()

    def finish(k):
        for d in (1, 2, 3):
            send_out(k, d).wait_recv()
        for m in range(SIDE):
            final[k, pl.ds(m, rows, stride=SIDE), :] = home[k, m]
        store(k).start()
        both = jnp.concatenate(split(final[k]), axis=1)
        term = lax.dot_general(
            both, drift_kernel[k], (((1,), (1,)), ((), ())), preferred_element_type=f32
        )
        stokes[...] += term[:, :LANES] + term[:, LANES:]

    relax(0)
    pl.semaphore_wait(barrier, tiles)
    for k in range(early):
        if k > 0:
            relax(k)
        launch(k)
        for side in range(2):
            send_first(k, y, side).start()
    ahead = 6
    for k in range(early, ahead - early + 1):
        relax(k)
        launch(k)
    for k in range(early):
        for d in (1, 3, 2):
            send_in(k, d).wait_recv()
            for side in range(2):
                send_first(k, lax.rem(y - d + SIDE, SIDE), side).start()
        if ahead - early + 1 + k < ahead:
            relax(ahead - early + 1 + k)
            launch(ahead - early + 1 + k)

    for each in side_loads:
        each.wait()
    prepare_masks()

    @pl.loop(0, chunks)
    def _(t):
        @pl.when(t + 3 + 3 < chunks)
        def _():
            relax(t + 3 + 3)
            launch(t + 3 + 3)

        @pl.when(t + 3 < chunks)
        def _():
            forward(t + 3)

        @pl.when(t == 0)
        def _():
            prepare_kernel()

        @pl.when(t == 1)
        def _():
            prepare_slots()

        @pl.when(t == 2)
        def _():
            prepare_zeta()

        set_out(t)

        @pl.when(t < early)
        def _():
            for side in range(2):
                for c in range(SIDE):
                    send_first(t, c, side).wait_recv()

        @pl.when(t >= early)
        def _():
            for side in range(2):
                send_halo(t, side).wait_recv()

        assemble(t)
        send_edge(t).start()

        sweep(t)

        @pl.when(t >= 2)
        def _():
            finish(t - 2)


    @pl.loop(chunks - 2, chunks)
    def _(k):
        finish(k)

    starts = [divmod(i * (drifts + 1), LANES) for i in range(slots)]
    both = jnp.concatenate(split(stokes[...]), axis=1)
    lane = lax.broadcasted_iota(jnp.int32, (per, LANES), 1)
    for step in range(parts):
        part = lax.rem(place // per + (2, 1, 3, 0)[step], parts)
        term = jnp.dot(
            placer[pl.ds(pl.multiple_of(part * per * slots, 2 * SUB), per * slots), :],
            both,
            preferred_element_type=f32,
        )
        packed = [jnp.zeros((per, LANES), f32) for _ in range(arrived.shape[1])]
        for i, (row, at) in enumerate(starts):
            mine = term[i * per : (i + 1) * per]
            mine = mine[:, :LANES] + mine[:, LANES:]
            if at:
                mine = pltpu.roll(mine, at, 1)
            end = at + drifts + 1
            packed[row] = jnp.where((lane >= at) & (lane < end), mine, packed[row])
            if end > LANES:
                packed[row + 1] = jnp.where(lane < end - LANES, mine, packed[row + 1])
        for row, values in enumerate(packed):
            posted[pl.ds(part * per, per), row, :] = values

        @pl.loop(1 if step == parts - 1 else 0, per)
        def _(d):
            post(part * per + lax.rem(place + d, per)).start()

    arrived[place] = posted[place]

    @pl.loop(0, chunks)
    def _(k):
        for d in (1, 2, 3):
            send_in(k, d).wait_send()
            send_out(k, d).wait_send()
        send_edge(k).wait_send()
        store(k).wait()

    @pl.loop(early, chunks)
    def _(k):
        for side in range(2):
            send_halo(k, side).wait_send()

    @pl.loop(0, early)
    def _(k):
        for side in range(2):
            for c in range(SIDE):
                send_first(k, c, side).wait_send()

    def all_of(ref, sem):
        some = ref.at[pl.ds(0, tiles - 1)]
        return pltpu.make_async_copy(some, some, sem)

    all_of(arrived, post_recv).wait()
    lane = lax.broadcasted_iota(jnp.int32, (tiles, LANES), 1)
    for i, (row, at) in enumerate(starts):
        taken = arrived[:, row, :]
        if at + drifts + 1 > LANES:
            taken = jnp.where(lane >= at, taken, arrived[:, row + 1, :])
        if at:
            taken = pltpu.roll(taken, LANES - at, 1)
        arrived_out[i * tiles : (i + 1) * tiles, :] = jnp.where(lane == drifts + 1, 1.0, taken)
    all_of(posted, post_send).wait()


def split(value):
    high = value.astype(jnp.bfloat16)
    return high, (value - high.astype(jnp.float32)).astype(jnp.bfloat16)


def ocean_kernel(profiles, waves, zeta, coriolis, velocity, out_hbm, velocity_out, give_sem):
    f32 = jnp.float32
    pieces = give_sem.shape[0]
    span = waves.shape[0] // pieces

    def give(i):
        at = pl.ds(i * span, span)
        return pltpu.make_async_copy(waves.at[at], out_hbm.at[at], give_sem.at[i])

    for i in range(pieces):
        give(i).start()
    levels, cols = zeta.shape
    drifts = 2 * levels
    rows_in = profiles[...]
    target = rows_in[:, drifts : drifts + 1]
    column = lax.broadcasted_iota(jnp.int32, (rows_in.shape[0], cols), 1).astype(f32) + 1.0
    chosen = (target == column).astype(jnp.bfloat16)
    summed = lax.dot_general(
        jnp.concatenate(split(rows_in), axis=1),
        chosen,
        (((0,), (0,)), ((), ())),
        preferred_element_type=f32,
    )
    summed = summed[:LANES] + summed[LANES:]
    count = jnp.maximum(summed[drifts + 1 : drifts + 2], 1.0)
    east_drift = summed[:levels] / count
    north_drift = summed[levels:drifts] / count
    spin = coriolis[...]
    turn = spin + zeta[...]
    east, north = velocity[0], velocity[1]
    velocity_out[0] = east + 0.25 * (spin * north + turn * north_drift)
    velocity_out[1] = north - 0.25 * (spin * east + turn * east_drift)
    for i in range(pieces):
        give(i).wait()


def per_device(
    spectrum,
    interaction,
    comp_speed,
    sea_mask,
    stokes_kernel,
    tile_owner,
    ocean_column,
    neighbours,
    coriolis,
    velocity,
):
    held, comps = spectrum.shape[1:]
    chunks = comps // LANES
    rows = held // SIDE
    tall = rows + 2 * SIDE
    tiles = lax.axis_size("pts")
    slots = 2 * held // tiles
    levels, cols = velocity.shape[2:]
    packed = -(-slots * (2 * levels + 1) // LANES)
    f32, bf16 = jnp.float32, jnp.bfloat16
    piece = pltpu.VMEM((chunks, SIDE, rows, LANES), f32)
    mask = pltpu.VMEM((tall * SUB, LANES), f32)
    vmem = pl.BlockSpec(memory_space=pltpu.VMEM)
    anywhere = pl.BlockSpec(memory_space=pl.ANY)
    hbm = pl.BlockSpec(memory_space=pltpu.HBM)
    dma = pltpu.SemaphoreType.DMA
    waves, profiles, zeta = pl.pallas_call(
        wave_kernel,
        out_shape=(
            jax.ShapeDtypeStruct((held, comps), f32),
            jax.ShapeDtypeStruct((tiles * slots, LANES), f32),
            jax.ShapeDtypeStruct((levels, cols), f32),
        ),
        in_specs=[hbm] * 9,
        out_specs=(anywhere, vmem, vmem),
        scratch_shapes=[
            pltpu.VMEM(sea_mask.shape, sea_mask.dtype),
            pltpu.VMEM(stokes_kernel.shape[::-1], f32),
            pltpu.VMEM((2, levels, cols), f32),
            pltpu.VMEM(comp_speed.shape, f32),
            pltpu.VMEM((1, held), jnp.int32),
            pltpu.VMEM((1, held), jnp.int32),
            pltpu.VMEM((neighbours.shape[2], cols), jnp.int32),
            pltpu.VMEM((chunks, held, LANES), f32),
            pltpu.VMEM((chunks, comps, LANES), bf16),
            pltpu.VMEM((held, comps), bf16),
            piece,
            piece,
            piece,
            piece,
            pltpu.VMEM((chunks, tall * SUB, LANES), f32),
            pltpu.VMEM(((tall + SUB) * SUB, LANES), f32),
            piece,
            piece,
            pltpu.VMEM((chunks, held, LANES), f32),
            pltpu.VMEM((2, tall * SUB, LANES), f32),
            pltpu.VMEM((2, tall * SUB, LANES), f32),
            mask,
            pltpu.VMEM((2 * rows, GC), f32),
            pltpu.VMEM((chunks, 2 * LANES, 2 * LANES), bf16),
            pltpu.VMEM((held, LANES), f32),
            pltpu.VMEM((tiles * slots, held), bf16),
            pltpu.VMEM((tiles, packed, LANES), f32),
            pltpu.VMEM((tiles, packed, LANES), f32),
            dma((2, chunks)),
            dma((7,)),
            dma((chunks,)),
            dma((chunks, 3)),
            dma((chunks, 3)),
            dma((chunks, 2)),
            dma((chunks, 2)),
            dma((chunks,)),
            dma((chunks,)),
            dma((chunks, 3)),
            dma((chunks, 3)),
            dma(()),
            dma(()),
            dma((3, SIDE, 2)),
            dma((3, SIDE, 2)),
        ],
        compiler_params=pltpu.CompilerParams(
            collective_id=0, has_side_effects=True, vmem_limit_bytes=36 << 20
        ),
        name="wave_step",
    )(
        *(
            pltpu.with_memory_space_constraint(each, pltpu.HBM)
            for each in (
                spectrum[0],
                interaction,
                sea_mask,
                stokes_kernel.T,
                velocity[0],
                comp_speed,
                tile_owner.reshape(1, held),
                ocean_column,
                neighbours[0].T,
            )
        )
    )
    spectrum_next, velocity_next = pl.pallas_call(
        ocean_kernel,
        out_shape=(
            jax.ShapeDtypeStruct((held, comps), f32),
            jax.ShapeDtypeStruct((2, levels, cols), f32),
        ),
        in_specs=[vmem] * 5,
        out_specs=(hbm, vmem),
        scratch_shapes=[dma((SIDE,))],
        compiler_params=pltpu.CompilerParams(vmem_limit_bytes=8 << 20),
        name="ocean_step",
    )(profiles, waves, zeta, coriolis, velocity[0])
    return (spectrum_next[None], velocity_next[None])


def solution(mesh):
    placed = (
        P("grid", "pts", None),
        P(),
        P(),
        P(),
        P(),
        P("grid", "pts", None),
        P("grid", "pts"),
        P("grid", "pts", None),
        P("grid", "pts"),
        P("grid", None, None, "pts"),
    )
    return jax.shard_map(
        per_device,
        mesh=mesh,
        in_specs=placed,
        out_specs=(P("grid", "pts", None), P("grid", None, None, "pts")),
        check_vma=False,
    )
```

```python
import jax
import jax.numpy as jnp
from jax import lax
from jax.experimental import pallas as pl
from jax.experimental.pallas import tpu as pltpu
from jax.sharding import PartitionSpec as P

MESH = pl.DeviceIdType.MESH
LANES = 128
SUB = 8
SIDE = 4
GC = 256


def wave_kernel(
    spec_hbm,
    inter_hbm,
    sea_hbm,
    kern_hbm,
    velocity_hbm,
    speed_hbm,
    owner_hbm,
    ocean_hbm,
    near_hbm,
    out_hbm,
    arrived_out,
    zeta,
    sea,
    kern,
    velocity,
    speed,
    owner,
    ocean,
    near,
    spec,
    inter,
    half,
    sent,
    own,
    left,
    right,
    wide,
    swept,
    back,
    home,
    final,
    mask_pos,
    mask_neg,
    mask_now,
    sea_rows,
    drift_kernel,
    stokes,
    placer,
    posted,
    arrived,
    load_sem,
    side_sem,
    store_sem,
    in_send,
    in_recv,
    halo_send,
    halo_recv,
    edge_send,
    edge_recv,
    out_send,
    out_recv,
    post_send,
    post_recv,
    first_send,
    first_recv,
):
    f32, bf16, i32 = jnp.float32, jnp.bfloat16, jnp.int32
    chunks, held = spec.shape[:2]
    rows = held // SIDE
    tall = rows + 2 * SIDE
    tiles = arrived.shape[0]
    drifts = kern.shape[0]
    slots = arrived_out.shape[0] // tiles
    parts = 4
    per = tiles // parts
    cols = near.shape[1]
    grid = lax.axis_index("grid")
    place = lax.axis_index("pts")
    y = lax.rem(place, SIDE)
    base = place - y
    rings = tiles // SIDE
    ring = place // SIDE
    peers = [base + lax.rem(y + d, SIDE) for d in (1, 2, 3)]
    lanes = lambda k: pl.ds(pl.multiple_of(k * LANES, LANES), LANES)

    def turned(k, r):
        return (r - (k + k // 3) + rings - 1) // rings

    def group(k):
        return lax.rem(y - turned(k, ring) + SIDE, SIDE)

    def block(k):
        return rings * group(k) + ring

    def beside(k, step):
        other = lax.rem(ring + step + rings, rings)
        across = (ring + step + rings) // rings - 1
        turn = across + turned(k, other) - turned(k, ring)
        return SIDE * other + lax.rem(y + turn + 2 * SIDE, SIDE)

    def load_spec(k):
        return pltpu.make_async_copy(spec_hbm.at[:, lanes(k)], spec.at[k], load_sem.at[0, k])

    def load_inter(k):
        return pltpu.make_async_copy(inter_hbm.at[:, lanes(k)], inter.at[k], load_sem.at[1, k])

    @pl.loop(0, chunks)
    def _(k):
        load_spec(k).start()

    load_inter(0).start()
    barrier = pltpu.get_barrier_semaphore()

    @pl.loop(1, tiles)
    def _(d):
        pl.semaphore_signal(
            barrier, inc=1, device_id={"pts": lax.rem(place + d, tiles)}, device_id_type=MESH
        )

    pl.semaphore_signal(barrier, inc=1, device_id={"grid": 1 - grid}, device_id_type=MESH)

    @pl.loop(1, chunks)
    def _(k):
        load_inter(k).start()

    side_loads = [
        pltpu.make_async_copy(source, target, side_sem.at[i])
        for i, (source, target) in enumerate(
            [
                (sea_hbm, sea),
                (kern_hbm, kern),
                (velocity_hbm, velocity),
                (speed_hbm, speed),
                (owner_hbm, owner),
                (ocean_hbm, ocean),
                (near_hbm, near),
            ]
        )
    ]
    for each in side_loads:
        each.start()

    for k in range(chunks):
        load_spec(k).wait()
        for m in range(SIDE):
            half[m * rows : (m + 1) * rows, k * LANES : (k + 1) * LANES] = spec[
                k, pl.ds(m, rows, stride=SIDE), :
            ].astype(bf16)

    def send_in(k, d):
        return pltpu.make_async_remote_copy(
            src_ref=sent.at[k, lax.rem(group(k) + d, SIDE)],
            dst_ref=own.at[k, y],
            send_sem=in_send.at[k, d - 1],
            recv_sem=in_recv.at[k, d - 1],
            device_id={"pts": peers[d - 1]},
            device_id_type=MESH,
        )

    def send_halo(k, side):
        return pltpu.make_async_remote_copy(
            src_ref=own.at[k],
            dst_ref=(left if side == 0 else right).at[k],
            send_sem=halo_send.at[k, side],
            recv_sem=halo_recv.at[k, side],
            device_id={"pts": beside(k, 1 if side == 0 else -1)},
            device_id_type=MESH,
        )

    early = first_send.shape[0]

    def send_first(k, c, side):
        return pltpu.make_async_remote_copy(
            src_ref=own.at[k, c],
            dst_ref=(left if side == 0 else right).at[k, c],
            send_sem=first_send.at[k, c, side],
            recv_sem=first_recv.at[k, c, side],
            device_id={"pts": beside(k, 1 if side == 0 else -1)},
            device_id_type=MESH,
        )

    def send_edge(k):
        at = pl.multiple_of((rows - (rows - SIDE) * grid) * SUB, SUB)
        to = pl.multiple_of((rows + SIDE) * SUB * grid, SUB)
        return pltpu.make_async_remote_copy(
            src_ref=wide.at[k, pl.ds(at, SIDE * SUB)],
            dst_ref=wide.at[k, pl.ds(to, SIDE * SUB)],
            send_sem=edge_send.at[k],
            recv_sem=edge_recv.at[k],
            device_id={"grid": 1 - grid},
            device_id_type=MESH,
        )

    def send_out(k, d):
        return pltpu.make_async_remote_copy(
            src_ref=back.at[k, lax.rem(y + d, SIDE)],
            dst_ref=home.at[k, group(k)],
            send_sem=out_send.at[k, d - 1],
            recv_sem=out_recv.at[k, d - 1],
            device_id={"pts": peers[d - 1]},
            device_id_type=MESH,
        )

    def post(peer):
        return pltpu.make_async_remote_copy(
            src_ref=posted.at[peer],
            dst_ref=arrived.at[place],
            send_sem=post_send,
            recv_sem=post_recv,
            device_id={"pts": peer},
            device_id_type=MESH,
        )

    def store(k):
        return pltpu.make_async_copy(final.at[k], out_hbm.at[:, lanes(k)], store_sem.at[k])

    def relax(k):
        load_inter(k).wait()
        mix = jnp.dot(half[...], inter[k], preferred_element_type=f32)
        grown = jnp.tanh(mix)
        for m in range(SIDE):
            local = spec[k, pl.ds(m, rows, stride=SIDE), :]
            sent[k, m] = local + 0.5 * local * grown[m * rows : (m + 1) * rows]
        own[k, y] = sent[k, group(k)]

    def launch(k):
        for d in (2, 1, 3):
            send_in(k, d).start()

    def forward(k):
        for d in (1, 2, 3):
            send_in(k, d).wait_recv()
        for side in range(2):
            send_halo(k, side).start()

    def prepare_masks():
        @pl.loop(0, rows)
        def _(r):
            pair = sea[:, pl.ds(pl.multiple_of(r * GC, GC), GC)].astype(f32)
            sea_rows[pl.ds(r, 1), :] = pair[0:1]
            sea_rows[pl.ds(r + rows, 1), :] = pair[1:2]

        row_at = lax.broadcasted_iota(i32, (tall, 2 * rows), 0) + (rows * grid - SIDE)
        row_of = lax.broadcasted_iota(i32, (tall, 2 * rows), 1)
        picked = jnp.dot(
            (row_at == row_of).astype(bf16),
            sea_rows[...].astype(bf16),
            preferred_element_type=f32,
        ).astype(bf16)
        column = lax.broadcasted_iota(i32, (GC, LANES), 0)
        for turn in range(2):
            start = SIDE * (rings * lax.rem(y - turn + SIDE, SIDE) + ring)
            for s in range(SUB):
                first = (column == start - SIDE + s).astype(bf16)
                second = (column == start + 7 - s).astype(bf16)
                mask_pos[turn, pl.ds(s, tall, stride=SUB), :] = jnp.dot(
                    picked, first, preferred_element_type=f32
                )
                mask_neg[turn, pl.ds(s, tall, stride=SUB), :] = jnp.dot(
                    picked, second, preferred_element_type=f32
                )

    def prepare_kernel():
        drift_kernel[...] = jnp.zeros_like(drift_kernel)
        for k in range(chunks):
            high, low = split(kern[:, k * LANES : (k + 1) * LANES])
            drift_kernel[k, 0:drifts, 0:LANES] = high
            drift_kernel[k, 0:drifts, LANES : 2 * LANES] = high
            drift_kernel[k, LANES : LANES + drifts, 0:LANES] = low

    def prepare_slots():
        down = lax.broadcasted_iota(i32, (held, held), 0)
        across = lax.broadcasted_iota(i32, (held, held), 1)
        owner_row = owner[...].astype(f32)
        owners = jnp.broadcast_to(owner_row, (held, held))
        owner_column = jnp.sum(jnp.where(down == across, owners, 0.0), axis=1, keepdims=True)
        earlier = (owners == owner_column) & (down < across)
        rank = jnp.sum(jnp.where(earlier, 1.0, 0.0), axis=0, keepdims=True)
        quarter = jnp.floor(owner_row / per)
        slot = (quarter * slots + rank) * per + (owner_row - quarter * per)
        for part in range(tiles * slots // LANES):
            at = lax.broadcasted_iota(i32, (LANES, held), 0) + part * LANES
            placer[part * LANES : (part + 1) * LANES, :] = (at.astype(f32) == slot).astype(bf16)
        wanted = jnp.broadcast_to(ocean[...].astype(f32) + 1.0, (held, held))
        target = jnp.sum(jnp.where(down == across, wanted, 0.0), axis=1, keepdims=True)
        lane = lax.broadcasted_iota(i32, (held, LANES), 1)
        stokes[...] = jnp.where(lane == drifts, target, 0.0)

    def prepare_zeta():
        column = lax.broadcasted_iota(i32, (cols, cols), 0)

        def apart(first, second):
            one = (near[first : first + 1, :] == column).astype(f32)
            two = (near[second : second + 1, :] == column).astype(f32)
            return (one - two).astype(bf16)

        def taken(flow, picker):
            high, low = split(flow)
            rest = (flow - high.astype(f32) - low.astype(f32)).astype(bf16)
            total = jnp.zeros(flow.shape, f32)
            for each in (high, low, rest):
                total += jnp.dot(each, picker, preferred_element_type=f32)
            return total

        zeta[...] = taken(velocity[1], apart(0, 1)) - taken(velocity[0], apart(2, 3))

    def set_out(k):
        pos = jnp.broadcast_to(speed[1:2, lanes(k)] > 0.0, (rows, LANES))
        for q in range(SIDE):
            wide[k, pl.ds(SIDE * SUB + SIDE + q, rows, stride=SUB), :] = jnp.where(
                pos, own[k, q], own[k, SIDE - 1 - q]
            )
        outside = pl.multiple_of((rows + SIDE) * SUB * grid, SUB)
        wide[k, pl.ds(outside, SIDE * SUB), :] = jnp.zeros((SIDE * SUB, LANES), f32)
        turn = turned(k, ring)
        each = jnp.broadcast_to(speed[1:2, lanes(k)], (SUB, LANES)) > 0.0

        @pl.loop(0, tall // SUB)
        def _(part):
            for u in range(SUB):
                at = pl.ds(pl.multiple_of((part * SUB + u) * SUB, SUB), SUB)
                mask_now[at, :] = jnp.where(each, mask_pos[turn, at, :], mask_neg[turn, at, :])

    def assemble(k):
        pos = jnp.broadcast_to(speed[1:2, lanes(k)] > 0.0, (rows, LANES))
        from_left = block(k) > 0
        from_right = block(k) < tiles - 1
        for s in range(SIDE):
            lower = jnp.where(from_left, left[k, s], 0.0)
            upper = jnp.where(from_right, right[k, SIDE - 1 - s], 0.0)
            wide[k, pl.ds(SIDE * SUB + s, rows, stride=SUB), :] = jnp.where(pos, lower, upper)

    def sweep(k):
        spread = lambda v: jnp.broadcast_to(v, (SUB, LANES))
        cx = speed[0:1, lanes(k)]
        cy = speed[1:2, lanes(k)]
        along = jnp.where(grid == 0, cx, -cx)
        behind_rate = spread(jnp.maximum(along, 0.0))
        front_rate = spread(jnp.maximum(-along, 0.0))
        side_rate = spread(jnp.abs(cy))
        keep = 1.0 - behind_rate - front_rate - side_rate
        zero = jnp.zeros((SUB, LANES), f32)

        def part(i, carry):
            held_rows = [list(pair) for pair in carry[0]]
            masks = list(carry[1])
            for u in range(SUB):
                r = i * SUB + u
                row = r + grid * (tall - 1 - 2 * r)
                at = pl.ds(pl.multiple_of(row * SUB, SUB), SUB)
                to = pl.ds(pl.multiple_of((row + grid * SUB) * SUB, SUB), SUB)
                value = wide[k, at, :]
                for stage in range(SIDE):
                    previous, current = held_rows[stage]
                    moved = (
                        keep * current
                        + behind_rate * previous
                        + front_rate * value
                        + side_rate * pltpu.roll(current, 1, 0)
                    )
                    held_rows[stage] = [current, value]
                    value = moved * masks[stage]
                swept[to, :] = value
                masks = [mask_now[at, :]] + masks[: SIDE - 1]
            return tuple(tuple(pair) for pair in held_rows), tuple(masks)

        start = (tuple((zero, zero) for _ in range(SIDE)), (zero,) * SIDE)
        nearly = lax.fori_loop(0, tall // SUB - 1, part, start)
        send_edge(k).wait_recv()
        part(tall // SUB - 1, nearly)
        wanted = jnp.broadcast_to(cy > 0.0, (rows, LANES))
        columns = [
            swept[pl.ds(2 * SIDE * SUB + SIDE + q, rows, stride=SUB), :] for q in range(SIDE)
        ]
        for c in range(SIDE):
            back[k, c] = jnp.where(wanted, columns[c], columns[SIDE - 1 - c])
        home[k, group(k)] = back[k, y]
        for d in (2, 1, 3):
            send_out(k, d).start()

    def finish(k):
        for d in (1, 2, 3):
            send_out(k, d).wait_recv()
        for m in range(SIDE):
            final[k, pl.ds(m, rows, stride=SIDE), :] = home[k, m]
        store(k).start()
        both = jnp.concatenate(split(final[k]), axis=1)
        term = lax.dot_general(
            both, drift_kernel[k], (((1,), (1,)), ((), ())), preferred_element_type=f32
        )
        stokes[...] += term[:, :LANES] + term[:, LANES:]

    relax(0)
    pl.semaphore_wait(barrier, tiles)
    for k in range(early):
        if k > 0:
            relax(k)
        launch(k)
        for side in range(2):
            send_first(k, y, side).start()
    ahead = 6
    for k in range(early, ahead - early + 1):
        relax(k)
        launch(k)
    for k in range(early):
        for d in (1, 3, 2):
            send_in(k, d).wait_recv()
            for side in range(2):
                send_first(k, lax.rem(y - d + SIDE, SIDE), side).start()
        if ahead - early + 1 + k < ahead:
            relax(ahead - early + 1 + k)
            launch(ahead - early + 1 + k)

    for each in side_loads:
        each.wait()
    prepare_masks()

    @pl.loop(0, chunks)
    def _(t):
        @pl.when(t + 3 + 3 < chunks)
        def _():
            relax(t + 3 + 3)
            launch(t + 3 + 3)

        @pl.when(t + 3 < chunks)
        def _():
            forward(t + 3)

        @pl.when(t == 0)
        def _():
            prepare_kernel()

        @pl.when(t == 1)
        def _():
            prepare_slots()

        @pl.when(t == 2)
        def _():
            prepare_zeta()

        set_out(t)

        @pl.when(t < early)
        def _():
            for side in range(2):
                for c in range(SIDE):
                    send_first(t, c, side).wait_recv()

        @pl.when(t >= early)
        def _():
            for side in range(2):
                send_halo(t, side).wait_recv()

        assemble(t)
        send_edge(t).start()

        sweep(t)

        @pl.when(t >= 2)
        def _():
            finish(t - 2)


    @pl.loop(chunks - 2, chunks)
    def _(k):
        finish(k)

    starts = [divmod(i * (drifts + 1), LANES) for i in range(slots)]
    both = jnp.concatenate(split(stokes[...]), axis=1)
    lane = lax.broadcasted_iota(jnp.int32, (per, LANES), 1)
    for step in range(parts):
        part = lax.rem(place // per + (2, 1, 3, 0)[step], parts)
        term = jnp.dot(
            placer[pl.ds(pl.multiple_of(part * per * slots, 2 * SUB), per * slots), :],
            both,
            preferred_element_type=f32,
        )
        packed = [jnp.zeros((per, LANES), f32) for _ in range(arrived.shape[1])]
        for i, (row, at) in enumerate(starts):
            mine = term[i * per : (i + 1) * per]
            mine = mine[:, :LANES] + mine[:, LANES:]
            if at:
                mine = pltpu.roll(mine, at, 1)
            end = at + drifts + 1
            packed[row] = jnp.where((lane >= at) & (lane < end), mine, packed[row])
            if end > LANES:
                packed[row + 1] = jnp.where(lane < end - LANES, mine, packed[row + 1])
        for row, values in enumerate(packed):
            posted[pl.ds(part * per, per), row, :] = values

        for d in range(1 if step == parts - 1 else 0, per):
            post(part * per + lax.rem(place + d, per)).start()

    arrived[place] = posted[place]

    @pl.loop(0, chunks)
    def _(k):
        for d in (1, 2, 3):
            send_in(k, d).wait_send()
            send_out(k, d).wait_send()
        send_edge(k).wait_send()
        store(k).wait()

    @pl.loop(early, chunks)
    def _(k):
        for side in range(2):
            send_halo(k, side).wait_send()

    @pl.loop(0, early)
    def _(k):
        for side in range(2):
            for c in range(SIDE):
                send_first(k, c, side).wait_send()

    def all_of(ref, sem):
        some = ref.at[pl.ds(0, tiles - 1)]
        return pltpu.make_async_copy(some, some, sem)

    all_of(arrived, post_recv).wait()
    lane = lax.broadcasted_iota(jnp.int32, (tiles, LANES), 1)
    for i, (row, at) in enumerate(starts):
        taken = arrived[:, row, :]
        if at + drifts + 1 > LANES:
            taken = jnp.where(lane >= at, taken, arrived[:, row + 1, :])
        if at:
            taken = pltpu.roll(taken, LANES - at, 1)
        arrived_out[i * tiles : (i + 1) * tiles, :] = jnp.where(lane == drifts + 1, 1.0, taken)
    all_of(posted, post_send).wait()


def split(value):
    high = value.astype(jnp.bfloat16)
    return high, (value - high.astype(jnp.float32)).astype(jnp.bfloat16)


def ocean_kernel(profiles, waves, zeta, coriolis, velocity, out_hbm, velocity_out, give_sem):
    f32 = jnp.float32
    pieces = give_sem.shape[0]
    span = waves.shape[0] // pieces

    def give(i):
        at = pl.ds(i * span, span)
        return pltpu.make_async_copy(waves.at[at], out_hbm.at[at], give_sem.at[i])

    for i in range(pieces):
        give(i).start()
    levels, cols = zeta.shape
    drifts = 2 * levels
    rows_in = profiles[...]
    target = rows_in[:, drifts : drifts + 1]
    column = lax.broadcasted_iota(jnp.int32, (rows_in.shape[0], cols), 1).astype(f32) + 1.0
    chosen = (target == column).astype(jnp.bfloat16)
    summed = lax.dot_general(
        jnp.concatenate(split(rows_in), axis=1),
        chosen,
        (((0,), (0,)), ((), ())),
        preferred_element_type=f32,
    )
    summed = summed[:LANES] + summed[LANES:]
    count = jnp.maximum(summed[drifts + 1 : drifts + 2], 1.0)
    east_drift = summed[:levels] / count
    north_drift = summed[levels:drifts] / count
    spin = coriolis[...]
    turn = spin + zeta[...]
    east, north = velocity[0], velocity[1]
    velocity_out[0] = east + 0.25 * (spin * north + turn * north_drift)
    velocity_out[1] = north - 0.25 * (spin * east + turn * east_drift)
    for i in range(pieces):
        give(i).wait()


def per_device(
    spectrum,
    interaction,
    comp_speed,
    sea_mask,
    stokes_kernel,
    tile_owner,
    ocean_column,
    neighbours,
    coriolis,
    velocity,
):
    held, comps = spectrum.shape[1:]
    chunks = comps // LANES
    rows = held // SIDE
    tall = rows + 2 * SIDE
    tiles = lax.axis_size("pts")
    slots = 2 * held // tiles
    levels, cols = velocity.shape[2:]
    packed = -(-slots * (2 * levels + 1) // LANES)
    f32, bf16 = jnp.float32, jnp.bfloat16
    piece = pltpu.VMEM((chunks, SIDE, rows, LANES), f32)
    mask = pltpu.VMEM((tall * SUB, LANES), f32)
    vmem = pl.BlockSpec(memory_space=pltpu.VMEM)
    anywhere = pl.BlockSpec(memory_space=pl.ANY)
    hbm = pl.BlockSpec(memory_space=pltpu.HBM)
    dma = pltpu.SemaphoreType.DMA
    waves, profiles, zeta = pl.pallas_call(
        wave_kernel,
        out_shape=(
            jax.ShapeDtypeStruct((held, comps), f32),
            jax.ShapeDtypeStruct((tiles * slots, LANES), f32),
            jax.ShapeDtypeStruct((levels, cols), f32),
        ),
        in_specs=[hbm] * 9,
        out_specs=(anywhere, vmem, vmem),
        scratch_shapes=[
            pltpu.VMEM(sea_mask.shape, sea_mask.dtype),
            pltpu.VMEM(stokes_kernel.shape[::-1], f32),
            pltpu.VMEM((2, levels, cols), f32),
            pltpu.VMEM(comp_speed.shape, f32),
            pltpu.VMEM((1, held), jnp.int32),
            pltpu.VMEM((1, held), jnp.int32),
            pltpu.VMEM((neighbours.shape[2], cols), jnp.int32),
            pltpu.VMEM((chunks, held, LANES), f32),
            pltpu.VMEM((chunks, comps, LANES), bf16),
            pltpu.VMEM((held, comps), bf16),
            piece,
            piece,
            piece,
            piece,
            pltpu.VMEM((chunks, tall * SUB, LANES), f32),
            pltpu.VMEM(((tall + SUB) * SUB, LANES), f32),
            piece,
            piece,
            pltpu.VMEM((chunks, held, LANES), f32),
            pltpu.VMEM((2, tall * SUB, LANES), f32),
            pltpu.VMEM((2, tall * SUB, LANES), f32),
            mask,
            pltpu.VMEM((2 * rows, GC), f32),
            pltpu.VMEM((chunks, 2 * LANES, 2 * LANES), bf16),
            pltpu.VMEM((held, LANES), f32),
            pltpu.VMEM((tiles * slots, held), bf16),
            pltpu.VMEM((tiles, packed, LANES), f32),
            pltpu.VMEM((tiles, packed, LANES), f32),
            dma((2, chunks)),
            dma((7,)),
            dma((chunks,)),
            dma((chunks, 3)),
            dma((chunks, 3)),
            dma((chunks, 2)),
            dma((chunks, 2)),
            dma((chunks,)),
            dma((chunks,)),
            dma((chunks, 3)),
            dma((chunks, 3)),
            dma(()),
            dma(()),
            dma((3, SIDE, 2)),
            dma((3, SIDE, 2)),
        ],
        compiler_params=pltpu.CompilerParams(
            collective_id=0, has_side_effects=True, vmem_limit_bytes=36 << 20
        ),
        name="wave_step",
    )(
        *(
            pltpu.with_memory_space_constraint(each, pltpu.HBM)
            for each in (
                spectrum[0],
                interaction,
                sea_mask,
                stokes_kernel.T,
                velocity[0],
                comp_speed,
                tile_owner.reshape(1, held),
                ocean_column,
                neighbours[0].T,
            )
        )
    )
    spectrum_next, velocity_next = pl.pallas_call(
        ocean_kernel,
        out_shape=(
            jax.ShapeDtypeStruct((held, comps), f32),
            jax.ShapeDtypeStruct((2, levels, cols), f32),
        ),
        in_specs=[vmem] * 5,
        out_specs=(hbm, vmem),
        scratch_shapes=[dma((SIDE,))],
        compiler_params=pltpu.CompilerParams(vmem_limit_bytes=8 << 20),
        name="ocean_step",
    )(profiles, waves, zeta, coriolis, velocity[0])
    return (spectrum_next[None], velocity_next[None])


def solution(mesh):
    placed = (
        P("grid", "pts", None),
        P(),
        P(),
        P(),
        P(),
        P("grid", "pts", None),
        P("grid", "pts"),
        P("grid", "pts", None),
        P("grid", "pts"),
        P("grid", None, None, "pts"),
    )
    return jax.shard_map(
        per_device,
        mesh=mesh,
        in_specs=placed,
        out_specs=(P("grid", "pts", None), P("grid", None, None, "pts")),
        check_vma=False,
    )
```
